256 devices in a mesh: rows: 64 (over z, y, core), feat: 4 (over x).
Axes of the slice: x: 4, y: 4, z: 8, core: 2. Of those that a mesh axis runs over, the one named last changes fastest.
Arguments:
- bin_codes: int32 [16, 983040], P(None, 'rows'), may hold values from 0 to 255
- node_ids: int32 [983040], P('rows'), may hold values from 0 to 7, as said below
- labels: float32 [983040], P('rows'), may hold values from -1 to 1, as said below
- weights: float32 [983040], P('rows'), as said below
- predictions: float32 [983040], P('rows'), may hold values from -6 to 6
- level3_feature: int32 [8], replicated, may hold values from 0 to 15
- level3_bin: int32 [8], replicated, may hold values from 64 to 191
- level4_feature: int32 [16], replicated, may hold values from 0 to 15
- level4_bin: int32 [16], replicated, may hold values from 64 to 191
Outputs:
- level3_hist: float32 [16, 16, 256], P('feat')
- level4_hist: float32 [16, 32, 256], P('feat')
- leaf_values: float32 [32], replicated
- new_predictions: float32 [983040], P('rows')
- new_weights: float32 [983040], P('rows')
The draws below stay inside these ranges and needn't reach their ends.
Inputs may be any that keep to these rules, and one draw needn't show every extreme that they name: `node_ids`: node ids of level 3. `labels`: every label is -1 or 1. `weights`: every weight is positive.
All inputs are finite; a program needn't handle non-finite values.
Results may differ from the reference program's by a relative error of at most 0.0003.
Values sent between devices are 32-bit elements; how exact they have to be, the bound alone decides.
A program may use at most 64 MiB of HBM per device.

```python
import jax
import jax.numpy as jnp
from jax import lax

FEATURES = 16
BINS = 256
NODES3 = 8
NODES4 = 16
LEAVES = 32
ROWS = 983040


def joint_rows(key):
    node_of = jax.random.randint(jax.random.fold_in(key, 11), (ROWS,), 0, NODES3)
    tilted = jax.random.uniform(jax.random.fold_in(key, 12), (NODES3,), minval=0.1, maxval=0.9)
    chance = jax.random.uniform(jax.random.fold_in(key, 13), (ROWS,))
    label_row = jnp.where(chance < tilted[node_of], 1.0, -1.0).astype(jnp.float32)
    return (node_of, label_row)


def draw_node_ids(key, part):
    return joint_rows(key)[0]


def draw_labels(key, part):
    return joint_rows(key)[1]


def draw_weights(key, part):
    position = jnp.arange(ROWS, dtype=jnp.float32) / ROWS
    ramped = 1.0 + 2.0 * position
    lowest = 0.2
    spread = jnp.exp(jax.random.uniform(jax.random.fold_in(key, 21), (ROWS,), minval=jnp.log(lowest), maxval=jnp.log(2.0)))
    return (ramped * spread * (NODES3 * BINS / ROWS)).astype(jnp.float32)


def touch_ends(entries, stream_key, least, top_value):
    longest = entries.shape.index(max(entries.shape))
    spots = []
    for shift in (0, 1):
        where = [jax.random.randint(jax.random.fold_in(stream_key, axis), (), 0, length) for axis, length in enumerate(entries.shape)]
        where[longest] = (where[longest] + shift) % entries.shape[longest]
        spots.append(tuple(where))
    return entries.at[spots[0]].set(least).at[spots[1]].set(top_value)


def shard_levels(rng, extent, split, smallest, high):
    loudness = 1.0
    for dim, shards_of in split:
        draws = jax.random.uniform(jax.random.fold_in(jax.random.fold_in(rng, 6), dim), (shards_of,), jnp.float32, smallest / len(split), high / len(split))
        loudness = loudness * jnp.repeat(jnp.exp(draws), extent[dim] // shards_of).reshape((-1,) + (1,) * (len(extent) - 1 - dim))
    return loudness


def gaussian(rng, shape, width, reach, cuts=(), held_as=jnp.bfloat16):
    values = jax.random.normal(rng, shape, jnp.float32) * width
    if len(cuts) > 0:
        values = shard_levels(rng, shape, cuts, -0.22, 0.18) * values
    return jnp.clip(values, min=-reach, max=reach).astype(held_as)


def setup_inputs(seed: int = 0) -> dict:
    key_list = jax.random.split(jax.random.key(seed), 10)
    bin_codes = touch_ends(jax.random.randint(key_list[0], (FEATURES, ROWS), 0, BINS), jax.random.fold_in(key_list[0], 1), 0, BINS - 1).astype(jnp.int32)
    node_ids = draw_node_ids(jax.random.fold_in(key_list[9], 71), 0)
    labels = draw_labels(jax.random.fold_in(key_list[9], 71), 0)
    weights = draw_weights(jax.random.fold_in(key_list[9], 71), 0)
    predictions = gaussian(key_list[4], (ROWS,), 1.0, 6.0, ((0, 64),), jnp.float32)
    level3_feature = touch_ends(jax.random.randint(key_list[5], (NODES3,), 0, FEATURES), jax.random.fold_in(key_list[5], 1), 0, FEATURES - 1).astype(jnp.int32)
    level3_bin = touch_ends(jax.random.randint(key_list[6], (NODES3,), BINS // 4, 3 * BINS // 4), jax.random.fold_in(key_list[6], 1), BINS // 4, (3 * BINS // 4) - 1).astype(jnp.int32)
    level4_feature = touch_ends(jax.random.randint(key_list[7], (NODES4,), 0, FEATURES), jax.random.fold_in(key_list[7], 1), 0, FEATURES - 1).astype(jnp.int32)
    level4_bin = touch_ends(jax.random.randint(key_list[8], (NODES4,), BINS // 4, 3 * BINS // 4), jax.random.fold_in(key_list[8], 1), BINS // 4, (3 * BINS // 4) - 1).astype(jnp.int32)
    return {"bin_codes": bin_codes, "node_ids": node_ids, "labels": labels, "weights": weights, "predictions": predictions, "level3_feature": level3_feature, "level3_bin": level3_bin, "level4_feature": level4_feature, "level4_bin": level4_bin}


def rounded(values):
    return lax.optimization_barrier(values.astype(jnp.bfloat16)).astype(jnp.float32)


def histogram(bin_codes, node_of, node_count, weight_round, signed_round):
    def one_feature(code_row):
        slot = node_of * BINS + code_row
        weight_sums = jax.ops.segment_sum(weight_round, slot, num_segments=node_count * BINS)
        signed_sums = jax.ops.segment_sum(signed_round, slot, num_segments=node_count * BINS)
        return jnp.concatenate([weight_sums.reshape(node_count, BINS), signed_sums.reshape(node_count, BINS)], axis=0)
    return lax.map(one_feature, bin_codes)


def routing(bin_codes, node_of, features, thresholds):
    chosen = features[node_of]
    cutoff = thresholds[node_of]
    picked = bin_codes[chosen, jnp.arange(node_of.shape[0], dtype=jnp.int32)]
    return (picked > cutoff).astype(jnp.int32)


def reference(bin_codes, node_ids, labels, weights, predictions, level3_feature, level3_bin, level4_feature, level4_bin):
    weight_round = rounded(weights)
    signed_round = rounded(weights * labels)
    level3_hist = histogram(bin_codes, node_ids, NODES3, weight_round, signed_round)
    node_four = 2 * node_ids + routing(bin_codes, node_ids, level3_feature, level3_bin)
    level4_hist = histogram(bin_codes, node_four, NODES4, weight_round, signed_round)
    leaf_of = 2 * node_four + routing(bin_codes, node_four, level4_feature, level4_bin)
    leaf_weight = jax.ops.segment_sum(weight_round, leaf_of, num_segments=LEAVES)
    leaf_signed = jax.ops.segment_sum(signed_round, leaf_of, num_segments=LEAVES)
    leaf_values = leaf_signed / (leaf_weight + 1.0)
    stepped = leaf_values[leaf_of]
    new_predictions = predictions + stepped
    raw_weights = weights * jnp.exp(-labels * stepped)
    new_weights = raw_weights * (ROWS / jnp.sum(raw_weights))
    return (level3_hist, level4_hist, leaf_values, new_predictions, new_weights)
```

```python
import functools

import jax
import jax.numpy as jnp
from jax import lax
from jax.experimental import pallas as pl
from jax.experimental.pallas import tpu as pltpu
from jax.sharding import PartitionSpec as P

FEATURES = 16
BINS = 256
NODES3 = 8
NODES4 = 16
LEAVES = 32
LANES = 128
GROUP = 8
MESH = pl.DeviceIdType.MESH
F32 = jnp.float32
BF16 = jnp.bfloat16


def flipped(index, mask):
    out = index
    for bit in (1, 2, 4):
        if mask & bit:
            out = out + bit * (1 - 2 * ((index // bit) % 2))
    return out


def tree_sum(parts):
    while len(parts) > 1:
        parts = [a + b for a, b in zip(parts[::2], parts[1::2])]
    return parts[0]


def kernel(
    total_rows,
    own_features,
    f3_ref,
    b3_ref,
    f4_ref,
    b4_ref,
    codes_ref,
    node_ref,
    label_ref,
    weight_ref,
    pred_ref,
    hist3_ref,
    hist4_ref,
    leaf_value_ref,
    new_pred_ref,
    new_weight_ref,
    key_ref,
    low_ref,
    wr_ref,
    sr_ref,
    leaf_ref,
    leafrow_ref,
    stat_ref,
    acc_ref,
    rs_ref,
    mid_ref,
    ar_ref,
    tot_ref,
    leaf_a_ref,
    leaf_b_ref,
    leaf_mid_ref,
    send_sem,
    rs_sem,
    ar_sem,
    ag_sem,
    leaf_send_sem,
    leaf_sem,
):
    tiles = node_ref.shape[0]
    steps = tiles // 8
    row = lax.axis_index("rows")
    feat = lax.axis_index("feat")
    group = row % GROUP
    plane = row // GROUP
    in_group = [(plane * GROUP + flipped(group, j), feat) for j in range(1, GROUP)]
    in_line = [(flipped(plane, j) * GROUP + group, feat) for j in range(1, GROUP)]

    barrier = pltpu.get_barrier_semaphore()
    for peer in in_group + in_line:
        pl.semaphore_signal(barrier, inc=1, device_id=peer, device_id_type=MESH)

    features3 = [f3_ref[i] for i in range(NODES3)]
    bins3 = [b3_ref[i] for i in range(NODES3)]
    features4 = [f4_ref[i] for i in range(NODES4)]
    bins4 = [b4_ref[i] for i in range(NODES4)]

    def lookup(where_of, tables):
        outs = [jnp.full((8, LANES), table[0], jnp.int32) for table in tables]
        for i in range(1, len(tables[0])):
            hit = where_of == i
            outs = [jnp.where(hit, table[i], out) for table, out in zip(tables, outs)]
        return outs

    def route(step, carry):
        rows = pl.ds(step * 8, 8)
        node = node_ref[rows, :]
        codes = [
            codes_ref[pl.ds((f // 8) * tiles * 8 + step * 64 + f % 8, 8, stride=8), :]
            for f in range(FEATURES)
        ]

        def side(node_of, features, bins):
            chosen, cutoff = lookup(node_of, [features, bins])
            picked = codes[0]
            for f in range(1, FEATURES):
                picked = jnp.where(chosen == f, codes[f], picked)
            return 2 * node_of + jnp.where(picked > cutoff, 1, 0)

        node4 = side(node, features3, bins3)
        leaf = side(node4, features4, bins4)
        leaf_ref[rows, :] = leaf
        leafrow_ref[rows, :] = leaf.astype(F32)
        for f in range(own_features):
            index = feat * own_features + f
            start = (index // 8) * (tiles * 8) + step * 64 + index % 8
            code = codes_ref[pl.ds(start, 8, stride=8), :]
            low_ref[f, rows, :] = (code & (LANES - 1)).astype(F32)
            key_ref[f, rows, :] = (node4 + NODES4 * (code >> 7)).astype(F32)
        weight = weight_ref[rows, :]
        label = label_ref[rows, :]
        rounded = weight.astype(BF16).astype(F32)
        wr_ref[rows, :] = rounded
        sr_ref[rows, :] = (weight * label).astype(BF16).astype(F32)
        rest = weight - rounded
        middle = rest.astype(BF16).astype(F32)
        low = rest - middle
        positive = label > 0.0
        for j, part in enumerate((rounded, middle, low)):
            stat_ref[pl.ds(step * 64 + j, 8, stride=8), :] = jnp.where(positive, part, 0.0)
            stat_ref[pl.ds(step * 64 + 3 + j, 8, stride=8), :] = jnp.where(positive, 0.0, part)
        for j in (6, 7):
            stat_ref[pl.ds(step * 64 + j, 8, stride=8), :] = jnp.zeros((8, LANES), F32)
        return carry

    lax.fori_loop(0, steps, route, 0)

    sub = lax.broadcasted_iota(jnp.int32, (16, LANES), 0).astype(F32)
    zero = jnp.zeros((16, LANES), BF16)
    one = jnp.ones((16, LANES), BF16)
    numbers = [(sub + 16 * i).astype(BF16) for i in range(8)]

    def spread(ref, *index):
        return jnp.broadcast_to(ref[index], (16, LANES)).astype(BF16)

    def dot_nt(a, b):
        return lax.dot_general(a, b, (((1,), (1,)), ((), ())), preferred_element_type=F32)

    def leaf_step(step, acc):
        left, right = [], []
        for i in range(8):
            t = step * 8 + i
            left.append(stat_ref[pl.ds(t * 8, 8), :].astype(BF16))
            at = spread(leafrow_ref, pl.ds(t, 1), slice(None))
            right.append(
                jnp.concatenate([jnp.where(at == numbers[k], one, zero) for k in range(2)], axis=0)
            )
        return acc + dot_nt(jnp.concatenate(left, axis=1), jnp.concatenate(right, axis=1))

    leaf_sums = lax.fori_loop(0, steps, leaf_step, jnp.zeros((8, LEAVES), F32))
    leaf_a_ref[0, :, :] = jnp.zeros((8, LANES), F32)
    leaf_a_ref[0, :, :LEAVES] = leaf_sums

    pl.semaphore_wait(barrier, 2 * (GROUP - 1))

    sends = []

    def send(source, target, sem, recv, peer):
        copy = pltpu.make_async_remote_copy(
            src_ref=source, dst_ref=target, send_sem=sem, recv_sem=recv, device_id=peer, device_id_type=MESH
        )
        copy.start()
        sends.append(copy)

    def arrived(ref, sem):
        pltpu.make_async_copy(ref, ref, sem).wait()

    for j in range(1, GROUP):
        send(leaf_a_ref.at[0], leaf_a_ref.at[j], leaf_send_sem.at[0, j - 1], leaf_sem.at[0], in_group[j - 1])

    def hist_step(f, step, acc):
        left, right = [], []
        for i in range(8):
            t = step * 8 + i
            key = spread(key_ref, f, pl.ds(t, 1), slice(None))
            low = spread(low_ref, f, pl.ds(t, 1), slice(None))
            wr = spread(wr_ref, pl.ds(t, 1), slice(None))
            sr = spread(sr_ref, pl.ds(t, 1), slice(None))
            blocks = []
            for hi in range(2):
                hit = key == numbers[hi]
                blocks += [jnp.where(hit, wr, zero), jnp.where(hit, sr, zero)]
            left.append(jnp.concatenate(blocks, axis=0))
            right.append(
                jnp.concatenate([jnp.where(low == numbers[k], one, zero) for k in range(8)], axis=0)
            )
        return acc + dot_nt(jnp.concatenate(left, axis=1), jnp.concatenate(right, axis=1))

    def compute(f):
        acc_ref[f, :, :] = lax.fori_loop(
            0, steps, functools.partial(hist_step, f), jnp.zeros((64, LANES), F32)
        )
        rs_ref[f, 0, :, :] = acc_ref[f, pl.ds(pl.multiple_of(group * 8, 8), 8), :]

    def scatter(f):
        for j in range(1, GROUP):
            rows = pl.ds(pl.multiple_of(flipped(group, j) * 8, 8), 8)
            send(acc_ref.at[f, rows], rs_ref.at[f, j], send_sem.at[f, 0, j - 1], rs_sem.at[f], in_group[j - 1])

    def exchange(f):
        arrived(rs_ref.at[f, pl.ds(1, GROUP - 1)], rs_sem.at[f])
        ar_ref[f, 0, :, :] = tree_sum([rs_ref[f, j] for j in range(GROUP)])
        for j in range(1, GROUP):
            send(ar_ref.at[f, 0], ar_ref.at[f, j], send_sem.at[f, 1, j - 1], ar_sem.at[f], in_line[j - 1])

    def gather(f):
        arrived(ar_ref.at[f, pl.ds(1, GROUP - 1)], ar_sem.at[f])
        mid_ref[f, :, :] = tree_sum([ar_ref[f, j] for j in range(GROUP)])
        rows = pl.ds(pl.multiple_of(group * 8, 8), 8)
        tot_ref[f, rows, :] = mid_ref[f, :, :]
        for j in range(1, GROUP):
            send(mid_ref.at[f], tot_ref.at[f, rows], send_sem.at[f, 2, j - 1], ag_sem.at[f], in_group[j - 1])

    compute(0)
    scatter(0)
    compute(1)
    scatter(1)

    arrived(leaf_a_ref.at[pl.ds(1, GROUP - 1)], leaf_sem.at[0])
    leaf_b_ref[0, :, :] = tree_sum([leaf_a_ref[j] for j in range(GROUP)])
    for j in range(1, GROUP):
        send(leaf_b_ref.at[0], leaf_b_ref.at[j], leaf_send_sem.at[1, j - 1], leaf_sem.at[1], in_line[j - 1])

    compute(2)
    scatter(2)
    exchange(0)
    compute(3)
    scatter(3)
    exchange(1)
    exchange(2)

    arrived(leaf_b_ref.at[pl.ds(1, GROUP - 1)], leaf_sem.at[1])
    leaf_mid_ref[...] = tree_sum([leaf_b_ref[j] for j in range(GROUP)])
    plus = leaf_mid_ref[0:1, :]
    minus = leaf_mid_ref[3:4, :]
    values = (plus - minus) / ((plus + minus) + 1.0)
    leaf_value_ref[...] = values
    all_plus = plus + (leaf_mid_ref[1:2, :] + leaf_mid_ref[2:3, :])
    all_minus = minus + (leaf_mid_ref[4:5, :] + leaf_mid_ref[5:6, :])
    grand = jnp.sum(all_plus * jnp.exp(-values) + all_minus * jnp.exp(values), axis=1, keepdims=True)
    scale = jnp.broadcast_to(total_rows / grand, (8, LANES))
    table = jnp.broadcast_to(values, (8, LANES))

    def update(step, carry):
        rows = pl.ds(step * 8, 8)
        stepped = jnp.take_along_axis(table, leaf_ref[rows, :], axis=1)
        new_pred_ref[rows, :] = pred_ref[rows, :] + stepped
        raw = weight_ref[rows, :] * jnp.exp(-label_ref[rows, :] * stepped)
        new_weight_ref[rows, :] = raw * scale
        return carry

    lax.fori_loop(0, steps, update, 0)

    exchange(3)
    for f in range(own_features):
        gather(f)
    for f in range(own_features):
        arrived(tot_ref.at[f, pl.ds(0, 8 * (GROUP - 1))], ag_sem.at[f])
        for hi in range(2):
            lanes = slice(hi * LANES, (hi + 1) * LANES)
            base = hi * 2 * NODES4
            hist4_ref[f, :, lanes] = tot_ref[f, base : base + 2 * NODES4, :]
            even = tot_ref[f, pl.ds(base, 2 * NODES3, stride=2), :]
            odd = tot_ref[f, pl.ds(base + 1, 2 * NODES3, stride=2), :]
            hist3_ref[f, :, lanes] = even + odd
    for copy in sends:
        copy.wait_send()


def on_device(bin_codes, node_ids, labels, weights, predictions, f3, b3, f4, b4):
    rows = node_ids.shape[0]
    tiles = rows // LANES
    total_rows = float(rows * lax.axis_size("rows"))
    own = FEATURES // lax.axis_size("feat")
    codes = bin_codes.reshape(FEATURES // 8, 8, tiles, LANES).transpose(0, 2, 1, 3)
    codes = codes.reshape(FEATURES * tiles, LANES)
    dense = [a.reshape(tiles, LANES) for a in (node_ids, labels, weights, predictions)]
    smem = pl.BlockSpec(memory_space=pltpu.SMEM)
    vmem = pl.BlockSpec(memory_space=pltpu.VMEM)
    outs = pl.pallas_call(
        functools.partial(kernel, total_rows, own),
        name="grow",
        in_specs=[smem] * 4 + [vmem] * 5,
        out_specs=[vmem] * 5,
        out_shape=[
            jax.ShapeDtypeStruct((own, 2 * NODES3, BINS), F32),
            jax.ShapeDtypeStruct((own, 2 * NODES4, BINS), F32),
            jax.ShapeDtypeStruct((1, LANES), F32),
            jax.ShapeDtypeStruct((tiles, LANES), F32),
            jax.ShapeDtypeStruct((tiles, LANES), F32),
        ],
        scratch_shapes=[
            pltpu.VMEM((own, tiles, LANES), F32),
            pltpu.VMEM((own, tiles, LANES), F32),
            pltpu.VMEM((tiles, LANES), F32),
            pltpu.VMEM((tiles, LANES), F32),
            pltpu.VMEM((tiles, LANES), jnp.int32),
            pltpu.VMEM((tiles, LANES), F32),
            pltpu.VMEM((tiles * 8, LANES), F32),
            pltpu.VMEM((own, 64, LANES), F32),
            pltpu.VMEM((own, GROUP, 8, LANES), F32),
            pltpu.VMEM((own, 8, LANES), F32),
            pltpu.VMEM((own, GROUP, 8, LANES), F32),
            pltpu.VMEM((own, 64, LANES), F32),
            pltpu.VMEM((GROUP, 8, LANES), F32),
            pltpu.VMEM((GROUP, 8, LANES), F32),
            pltpu.VMEM((8, LANES), F32),
            pltpu.SemaphoreType.DMA((own, 3, GROUP - 1)),
            pltpu.SemaphoreType.DMA((own,)),
            pltpu.SemaphoreType.DMA((own,)),
            pltpu.SemaphoreType.DMA((own,)),
            pltpu.SemaphoreType.DMA((2, GROUP - 1)),
            pltpu.SemaphoreType.DMA((2,)),
        ],
        compiler_params=pltpu.CompilerParams(collective_id=0, has_side_effects=True),
    )(f3, b3, f4, b4, codes, *dense)
    hist3, hist4, leaf_values, new_pred, new_weight = outs
    return (
        hist3,
        hist4,
        leaf_values[0, :LEAVES],
        new_pred.reshape(rows),
        new_weight.reshape(rows),
    )


def solution(mesh):
    placed = (P(None, "rows"), P("rows"), P("rows"), P("rows"), P("rows"), P(), P(), P(), P())
    return jax.shard_map(
        on_device,
        mesh=mesh,
        in_specs=placed,
        out_specs=(P("feat", None, None), P("feat", None, None), P(), P("rows"), P("rows")),
        check_vma=False,
    )
```

```python
import functools

import jax
import jax.numpy as jnp
from jax import lax
from jax.experimental import pallas as pl
from jax.experimental.pallas import tpu as pltpu
from jax.sharding import PartitionSpec as P

FEATURES = 16
BINS = 256
NODES3 = 8
NODES4 = 16
LEAVES = 32
LANES = 128
CHUNKS = 3
GROUP = 8
MESH = pl.DeviceIdType.MESH
F32 = jnp.float32
BF16 = jnp.bfloat16


def flipped(index, mask):
    out = index
    for bit in (1, 2, 4):
        if mask & bit:
            out = out + bit * (1 - 2 * ((index // bit) % 2))
    return out


def tree_sum(parts):
    while len(parts) > 1:
        parts = [a + b for a, b in zip(parts[::2], parts[1::2])]
    return parts[0]


def kernel(
    total_rows,
    own_features,
    f3_hbm,
    b3_hbm,
    f4_hbm,
    b4_hbm,
    codes_hbm,
    node_hbm,
    label_hbm,
    weight_hbm,
    pred_hbm,
    hist3_ref,
    hist4_ref,
    leaf_value_ref,
    new_pred_ref,
    new_weight_ref,
    f3_ref,
    b3_ref,
    f4_ref,
    b4_ref,
    codes_ref,
    node_ref,
    label_ref,
    weight_ref,
    pred_ref,
    key_ref,
    low_ref,
    wr_ref,
    sr_ref,
    leaf_ref,
    leafrow_ref,
    stat_ref,
    acc_ref,
    rs_ref,
    mid_ref,
    ar_ref,
    tot_ref,
    leaf_a_ref,
    leaf_b_ref,
    leaf_mid_ref,
    send_sem,
    rs_sem,
    ar_sem,
    ag_sem,
    leaf_send_sem,
    leaf_sem,
    in_sem,
    code_sem,
):
    tiles = node_hbm.shape[0]
    steps = tiles // 8
    row = lax.axis_index("rows")
    feat = lax.axis_index("feat")
    group = row % GROUP
    plane = row // GROUP
    in_group = [(plane * GROUP + flipped(group, j), feat) for j in range(1, GROUP)]
    in_line = [(flipped(plane, j) * GROUP + group, feat) for j in range(1, GROUP)]

    barrier = pltpu.get_barrier_semaphore()
    with jax.named_scope('signal'):
        for peer in in_group + in_line:
            pl.semaphore_signal(barrier, inc=1, device_id=peer, device_id_type=MESH)

    def fetch(source, target, sem):
        copy = pltpu.make_async_copy(source, target, sem)
        copy.start()
        return copy

    part = tiles * 8 // CHUNKS
    pieces = [pl.ds(c * part, part) for c in range(CHUNKS)]
    small = [
        (f3_hbm, f3_ref),
        (b3_hbm, b3_ref),
        (f4_hbm, f4_ref),
        (b4_hbm, b4_ref),
        (node_hbm, node_ref),
        (label_hbm, label_ref),
        (weight_hbm, weight_ref),
        (pred_hbm, pred_ref),
    ]
    ready = [fetch(a, b, in_sem.at[i]) for i, (a, b) in enumerate(small[:5])]
    code_ready = []
    for c in range(CHUNKS):
        code_ready.append(fetch(codes_hbm.at[:, pieces[c]], codes_ref.at[:, pieces[c]], code_sem.at[c]))
        if c == 0:
            ready += [fetch(a, b, in_sem.at[5 + i]) for i, (a, b) in enumerate(small[5:])]
    with jax.named_scope('inwait'):
        for copy in ready:
            copy.wait()

    features3 = [f3_ref[i] for i in range(NODES3)]
    bins3 = [b3_ref[i] for i in range(NODES3)]
    features4 = [f4_ref[i] for i in range(NODES4)]
    bins4 = [b4_ref[i] for i in range(NODES4)]

    def lookup(where_of, tables):
        outs = [jnp.full((8, LANES), table[0], jnp.int32) for table in tables]
        for i in range(1, len(tables[0])):
            hit = where_of == i
            outs = [jnp.where(hit, table[i], out) for table, out in zip(tables, outs)]
        return outs

    def route(step, carry):
        rows = pl.ds(step * 8, 8)
        node = node_ref[rows, :]
        codes = [
            codes_ref[f // 8, pl.ds(step * 64 + f % 8, 8, stride=8), :]
            for f in range(FEATURES)
        ]

        def side(node_of, features, bins):
            chosen, cutoff = lookup(node_of, [features, bins])
            picked = codes[0]
            for f in range(1, FEATURES):
                picked = jnp.where(chosen == f, codes[f], picked)
            return 2 * node_of + jnp.where(picked > cutoff, 1, 0)

        node4 = side(node, features3, bins3)
        leaf = side(node4, features4, bins4)
        leaf_ref[rows, :] = leaf
        leafrow_ref[rows, :] = leaf.astype(F32)
        for f in range(own_features):
            index = feat * own_features + f
            code = codes_ref[index // 8, pl.ds(step * 64 + index % 8, 8, stride=8), :]
            low_ref[f, rows, :] = (code & (LANES - 1)).astype(F32)
            key_ref[f, rows, :] = (node4 + NODES4 * (code >> 7)).astype(F32)
        weight = weight_ref[rows, :]
        label = label_ref[rows, :]
        rounded = weight.astype(BF16).astype(F32)
        wr_ref[rows, :] = rounded
        sr_ref[rows, :] = (weight * label).astype(BF16).astype(F32)
        rest = weight - rounded
        middle = rest.astype(BF16).astype(F32)
        low = rest - middle
        positive = label > 0.0
        for j, part in enumerate((rounded, middle, low)):
            stat_ref[pl.ds(step * 64 + j, 8, stride=8), :] = jnp.where(positive, part, 0.0)
            stat_ref[pl.ds(step * 64 + 3 + j, 8, stride=8), :] = jnp.where(positive, 0.0, part)
        for j in (6, 7):
            stat_ref[pl.ds(step * 64 + j, 8, stride=8), :] = jnp.zeros((8, LANES), F32)
        return carry

    with jax.named_scope('route'):
        for c in range(CHUNKS):
            code_ready[c].wait()
            lax.fori_loop(c * steps // CHUNKS, (c + 1) * steps // CHUNKS, route, 0, unroll=5)

    sub = lax.broadcasted_iota(jnp.int32, (16, LANES), 0).astype(F32)
    zero = jnp.zeros((16, LANES), BF16)
    one = jnp.ones((16, LANES), BF16)
    numbers = [(sub + 16 * i).astype(BF16) for i in range(8)]

    def spread(ref, *index):
        return jnp.broadcast_to(ref[index], (16, LANES)).astype(BF16)

    def dot_nt(a, b):
        return lax.dot_general(a, b, (((1,), (1,)), ((), ())), preferred_element_type=F32)

    def leaf_step(step, acc):
        left, right = [], []
        for i in range(8):
            t = step * 8 + i
            left.append(stat_ref[pl.ds(t * 8, 8), :].astype(BF16))
            at = spread(leafrow_ref, pl.ds(t, 1), slice(None))
            right.append(
                jnp.concatenate([jnp.where(at == numbers[k], one, zero) for k in range(2)], axis=0)
            )
        return acc + dot_nt(jnp.concatenate(left, axis=1), jnp.concatenate(right, axis=1))

    sends = []

    def send(source, target, sem, recv, peer):
        copy = pltpu.make_async_remote_copy(
            src_ref=source, dst_ref=target, send_sem=sem, recv_sem=recv, device_id=peer, device_id_type=MESH
        )
        copy.start()
        sends.append(copy)

    def arrived(ref, sem):
        pltpu.make_async_copy(ref, ref, sem).wait()

    def leaf_scatter():
        leaf_sums = lax.fori_loop(0, steps, leaf_step, jnp.zeros((8, LEAVES), F32), unroll=5)
        leaf_a_ref[0, :, :] = jnp.zeros((8, LANES), F32)
        leaf_a_ref[0, :, :LEAVES] = leaf_sums
        for j in range(1, GROUP):
            send(leaf_a_ref.at[0], leaf_a_ref.at[j], leaf_send_sem.at[0, j - 1], leaf_sem.at[0], in_group[j - 1])

    def leaf_exchange():
        with jax.named_scope('leafwait1'):
            arrived(leaf_a_ref.at[pl.ds(1, GROUP - 1)], leaf_sem.at[0])
        leaf_b_ref[0, :, :] = tree_sum([leaf_a_ref[j] for j in range(GROUP)])
        for j in range(1, GROUP):
            send(leaf_b_ref.at[0], leaf_b_ref.at[j], leaf_send_sem.at[1, j - 1], leaf_sem.at[1], in_line[j - 1])

    def hist_step(f, step, acc):
        left, right = [], []
        for i in range(8):
            t = step * 8 + i
            key = spread(key_ref, f, pl.ds(t, 1), slice(None))
            low = spread(low_ref, f, pl.ds(t, 1), slice(None))
            wr = spread(wr_ref, pl.ds(t, 1), slice(None))
            sr = spread(sr_ref, pl.ds(t, 1), slice(None))
            blocks = []
            for hi in range(2):
                hit = key == numbers[hi]
                blocks += [jnp.where(hit, wr, zero), jnp.where(hit, sr, zero)]
            left.append(jnp.concatenate(blocks, axis=0))
            right.append(
                jnp.concatenate([jnp.where(low == numbers[k], one, zero) for k in range(8)], axis=0)
            )
        return acc + dot_nt(jnp.concatenate(right, axis=1), jnp.concatenate(left, axis=1))

    def compute(f):
        acc_ref[f, :, :] = lax.fori_loop(
            0, steps, functools.partial(hist_step, f), jnp.zeros((LANES, 64), F32), unroll=5
        ).T
        rs_ref[f, 0, :, :] = acc_ref[f, pl.ds(pl.multiple_of(group * 8, 8), 8), :]

    def scatter(f):
        for j in range(1, GROUP):
            rows = pl.ds(pl.multiple_of(flipped(group, j) * 8, 8), 8)
            send(acc_ref.at[f, rows], rs_ref.at[f, j], send_sem.at[f, 0, j - 1], rs_sem.at[f], in_group[j - 1])

    def exchange(f):
        arrived(rs_ref.at[f, pl.ds(1, GROUP - 1)], rs_sem.at[f])
        ar_ref[f, 0, :, :] = tree_sum([rs_ref[f, j] for j in range(GROUP)])
        for j in range(1, GROUP):
            send(ar_ref.at[f, 0], ar_ref.at[f, j], send_sem.at[f, 1, j - 1], ar_sem.at[f], in_line[j - 1])

    def gather(f):
        arrived(ar_ref.at[f, pl.ds(1, GROUP - 1)], ar_sem.at[f])
        mid_ref[f, :, :] = tree_sum([ar_ref[f, j] for j in range(GROUP)])
        rows = pl.ds(pl.multiple_of(group * 8, 8), 8)
        tot_ref[f, rows, :] = mid_ref[f, :, :]
        for j in range(1, GROUP):
            send(mid_ref.at[f], tot_ref.at[f, rows], send_sem.at[f, 2, j - 1], ag_sem.at[f], in_group[j - 1])

    with jax.named_scope('compute0'):
        compute(0)
    with jax.named_scope('compute1'):
        compute(1)
    with jax.named_scope('barwait'):
        pl.semaphore_wait(barrier, 2 * (GROUP - 1))
    with jax.named_scope('scatter0'):
        scatter(0)
    with jax.named_scope('scatter1'):
        scatter(1)
    with jax.named_scope('compute2'):
        compute(2)
    with jax.named_scope('scatter2'):
        scatter(2)
    with jax.named_scope('compute3'):
        compute(3)
    with jax.named_scope('scatter3'):
        scatter(3)
    with jax.named_scope('exchange0'):
        exchange(0)
    with jax.named_scope('exchange1'):
        exchange(1)
    with jax.named_scope('leaf_scatter'):
        leaf_scatter()
    with jax.named_scope('exchange2'):
        exchange(2)
    with jax.named_scope('exchange3'):
        exchange(3)
    with jax.named_scope('leaf_exchange'):
        leaf_exchange()
    with jax.named_scope('gather0'):
        gather(0)
    with jax.named_scope('gather1'):
        gather(1)
    with jax.named_scope('gather2'):
        gather(2)
    with jax.named_scope('gather3'):
        gather(3)
    with jax.named_scope('leafwait2'):
        arrived(leaf_b_ref.at[pl.ds(1, GROUP - 1)], leaf_sem.at[1])
    leaf_mid_ref[...] = tree_sum([leaf_b_ref[j] for j in range(GROUP)])
    plus = leaf_mid_ref[0:1, :]
    minus = leaf_mid_ref[3:4, :]
    values = (plus - minus) / ((plus + minus) + 1.0)
    leaf_value_ref[...] = values
    all_plus = plus + (leaf_mid_ref[1:2, :] + leaf_mid_ref[2:3, :])
    all_minus = minus + (leaf_mid_ref[4:5, :] + leaf_mid_ref[5:6, :])
    grand = jnp.sum(all_plus * jnp.exp(-values) + all_minus * jnp.exp(values), axis=1, keepdims=True)
    scale = jnp.broadcast_to(total_rows / grand, (8, LANES))
    table = jnp.broadcast_to(values, (8, LANES))

    def update(step, carry):
        rows = pl.ds(step * 8, 8)
        stepped = jnp.take_along_axis(table, leaf_ref[rows, :], axis=1)
        new_pred_ref[rows, :] = pred_ref[rows, :] + stepped
        raw = weight_ref[rows, :] * jnp.exp(-label_ref[rows, :] * stepped)
        new_weight_ref[rows, :] = raw * scale
        return carry

    with jax.named_scope('update'):
        lax.fori_loop(0, steps, update, 0, unroll=5)

    for f in range(own_features):
        with jax.named_scope('agwait'):
            arrived(tot_ref.at[f, pl.ds(0, 8 * (GROUP - 1))], ag_sem.at[f])
        for hi in range(2):
            lanes = slice(hi * LANES, (hi + 1) * LANES)
            base = hi * 2 * NODES4
            hist4_ref[f, :, lanes] = tot_ref[f, base : base + 2 * NODES4, :]
            even = tot_ref[f, pl.ds(base, 2 * NODES3, stride=2), :]
            odd = tot_ref[f, pl.ds(base + 1, 2 * NODES3, stride=2), :]
            hist3_ref[f, :, lanes] = even + odd
    with jax.named_scope('sendwait'):
        for copy in sends:
            copy.wait_send()


def store_kernel(h3, h4, values, pred, weight, h3_out, h4_out, values_out, pred_out, weight_out, sem):
    pairs = [(h3, h3_out), (h4, h4_out), (pred, pred_out), (weight, weight_out)]
    copies = [pltpu.make_async_copy(a, b, sem.at[i]) for i, (a, b) in enumerate(pairs)]
    for copy in copies:
        copy.start()
    values_out[...] = values[0, :LEAVES]
    for copy in copies:
        copy.wait()


def on_device(bin_codes, node_ids, labels, weights, predictions, f3, b3, f4, b4):
    rows = node_ids.shape[0]
    tiles = rows // LANES
    total_rows = float(rows * lax.axis_size("rows"))
    own = FEATURES // lax.axis_size("feat")
    codes = bin_codes.reshape(FEATURES // 8, 8, tiles, LANES).transpose(0, 2, 1, 3)
    codes = codes.reshape(FEATURES // 8, tiles * 8, LANES)
    dense = [a.reshape(tiles, LANES) for a in (node_ids, labels, weights, predictions)]
    held = pl.BlockSpec(memory_space=pltpu.HBM)
    vmem = pl.BlockSpec(memory_space=pltpu.VMEM)
    outs = pl.pallas_call(
        functools.partial(kernel, total_rows, own),
        name="grow",
        in_specs=[held] * 9,
        out_specs=[vmem] * 5,
        out_shape=[
            jax.ShapeDtypeStruct((own, 2 * NODES3, BINS), F32),
            jax.ShapeDtypeStruct((own, 2 * NODES4, BINS), F32),
            jax.ShapeDtypeStruct((1, LANES), F32),
            jax.ShapeDtypeStruct((tiles, LANES), F32),
            jax.ShapeDtypeStruct((tiles, LANES), F32),
        ],
        scratch_shapes=[
            pltpu.SMEM((NODES3,), jnp.int32),
            pltpu.SMEM((NODES3,), jnp.int32),
            pltpu.SMEM((NODES4,), jnp.int32),
            pltpu.SMEM((NODES4,), jnp.int32),
            pltpu.VMEM(codes.shape, jnp.int32),
            pltpu.VMEM((tiles, LANES), jnp.int32),
            pltpu.VMEM((tiles, LANES), F32),
            pltpu.VMEM((tiles, LANES), F32),
            pltpu.VMEM((tiles, LANES), F32),
            pltpu.VMEM((own, tiles, LANES), F32),
            pltpu.VMEM((own, tiles, LANES), F32),
            pltpu.VMEM((tiles, LANES), F32),
            pltpu.VMEM((tiles, LANES), F32),
            pltpu.VMEM((tiles, LANES), jnp.int32),
            pltpu.VMEM((tiles, LANES), F32),
            pltpu.VMEM((tiles * 8, LANES), F32),
            pltpu.VMEM((own, 64, LANES), F32),
            pltpu.VMEM((own, GROUP, 8, LANES), F32),
            pltpu.VMEM((own, 8, LANES), F32),
            pltpu.VMEM((own, GROUP, 8, LANES), F32),
            pltpu.VMEM((own, 64, LANES), F32),
            pltpu.VMEM((GROUP, 8, LANES), F32),
            pltpu.VMEM((GROUP, 8, LANES), F32),
            pltpu.VMEM((8, LANES), F32),
            pltpu.SemaphoreType.DMA((own, 3, GROUP - 1)),
            pltpu.SemaphoreType.DMA((own,)),
            pltpu.SemaphoreType.DMA((own,)),
            pltpu.SemaphoreType.DMA((own,)),
            pltpu.SemaphoreType.DMA((2, GROUP - 1)),
            pltpu.SemaphoreType.DMA((2,)),
            pltpu.SemaphoreType.DMA((8,)),
            pltpu.SemaphoreType.DMA((CHUNKS,)),
        ],
        compiler_params=pltpu.CompilerParams(collective_id=0, has_side_effects=True, vmem_limit_bytes=16 << 20),
    )(*[pltpu.with_memory_space_constraint(a, pltpu.HBM) for a in (f3, b3, f4, b4, codes, *dense)])
    hbm = pl.BlockSpec(memory_space=pl.ANY)
    like = [jax.ShapeDtypeStruct(a.shape, F32) for a in outs]
    like[2] = jax.ShapeDtypeStruct((LEAVES,), F32)
    hist3, hist4, leaf_values, new_pred, new_weight = pl.pallas_call(
        store_kernel,
        name="store",
        in_specs=[hbm, hbm, vmem, hbm, hbm],
        out_specs=[hbm, hbm, vmem, hbm, hbm],
        out_shape=like,
        scratch_shapes=[pltpu.SemaphoreType.DMA((4,))],
        compiler_params=pltpu.CompilerParams(vmem_limit_bytes=1 << 20),
    )(*outs)
    return hist3, hist4, leaf_values, new_pred.reshape(rows), new_weight.reshape(rows)


def solution(mesh):
    placed = (P(None, "rows"), P("rows"), P("rows"), P("rows"), P("rows"), P(), P(), P(), P())
    return jax.shard_map(
        on_device,
        mesh=mesh,
        in_specs=placed,
        out_specs=(P("feat", None, None), P("feat", None, None), P(), P("rows"), P("rows")),
        check_vma=False,
    )
```

```python
import functools

import jax
import jax.numpy as jnp
from jax import lax
from jax.experimental import pallas as pl
from jax.experimental.pallas import tpu as pltpu
from jax.sharding import PartitionSpec as P

FEATURES = 16
BINS = 256
NODES3 = 8
NODES4 = 16
LEAVES = 32
LANES = 128
CHUNKS = 3
GROUP = 8
MESH = pl.DeviceIdType.MESH
F32 = jnp.float32
BF16 = jnp.bfloat16


def flipped(index, mask):
    out = index
    for bit in (1, 2, 4):
        if mask & bit:
            out = out + bit * (1 - 2 * ((index // bit) % 2))
    return out


def tree_sum(parts):
    while len(parts) > 1:
        parts = [a + b for a, b in zip(parts[::2], parts[1::2])]
    return parts[0]


def kernel(
    total_rows,
    own_features,
    f3_hbm,
    b3_hbm,
    f4_hbm,
    b4_hbm,
    codes_hbm,
    node_hbm,
    label_hbm,
    weight_hbm,
    pred_hbm,
    hist3_ref,
    hist4_ref,
    leaf_value_ref,
    new_pred_ref,
    new_weight_ref,
    f3_ref,
    b3_ref,
    f4_ref,
    b4_ref,
    codes_ref,
    node_ref,
    label_ref,
    weight_ref,
    pred_ref,
    key_ref,
    low_ref,
    wr_ref,
    sr_ref,
    leaf_ref,
    leafrow_ref,
    stat_ref,
    acc_ref,
    rs_ref,
    mid_ref,
    ar_ref,
    tot_ref,
    leaf_a_ref,
    leaf_b_ref,
    leaf_mid_ref,
    send_sem,
    rs_sem,
    ar_sem,
    ag_sem,
    leaf_send_sem,
    leaf_sem,
    in_sem,
    code_sem,
):
    tiles = node_hbm.shape[0]
    steps = tiles // 8
    row = lax.axis_index("rows")
    feat = lax.axis_index("feat")
    group = row % GROUP
    plane = row // GROUP
    in_group = [(plane * GROUP + flipped(group, j), feat) for j in range(1, GROUP)]
    in_line = [(flipped(plane, j) * GROUP + group, feat) for j in range(1, GROUP)]

    barrier = pltpu.get_barrier_semaphore()
    with jax.named_scope('signal'):
        for peer in in_group + in_line:
            pl.semaphore_signal(barrier, inc=1, device_id=peer, device_id_type=MESH)

    def fetch(source, target, sem):
        copy = pltpu.make_async_copy(source, target, sem)
        copy.start()
        return copy

    part = tiles * 8 // CHUNKS
    pieces = [pl.ds(c * part, part) for c in range(CHUNKS)]
    small = [
        (f3_hbm, f3_ref),
        (b3_hbm, b3_ref),
        (f4_hbm, f4_ref),
        (b4_hbm, b4_ref),
        (node_hbm, node_ref),
        (label_hbm, label_ref),
        (weight_hbm, weight_ref),
        (pred_hbm, pred_ref),
    ]
    ready = [fetch(a, b, in_sem.at[i]) for i, (a, b) in enumerate(small[:5])]
    for c in range(CHUNKS):
        fetch(codes_hbm.at[:, pieces[c]], codes_ref.at[:, pieces[c]], code_sem.at[c])
        if c == 0:
            ready += [fetch(a, b, in_sem.at[5 + i]) for i, (a, b) in enumerate(small[5:])]
    for i, copy in enumerate(ready):
        with jax.named_scope('inwait%d' % i):
            copy.wait()

    features3 = [f3_ref[i] for i in range(NODES3)]
    bins3 = [b3_ref[i] for i in range(NODES3)]
    features4 = [f4_ref[i] for i in range(NODES4)]
    bins4 = [b4_ref[i] for i in range(NODES4)]

    def lookup(where_of, tables):
        outs = [jnp.full((8, LANES), table[0], jnp.int32) for table in tables]
        for i in range(1, len(tables[0])):
            hit = where_of == i
            outs = [jnp.where(hit, table[i], out) for table, out in zip(tables, outs)]
        return outs

    def route(step, carry):
        rows = pl.ds(step * 8, 8)
        node = node_ref[rows, :]
        codes = [
            codes_ref[f // 8, pl.ds(step * 64 + f % 8, 8, stride=8), :]
            for f in range(FEATURES)
        ]

        def side(node_of, features, bins):
            chosen, cutoff = lookup(node_of, [features, bins])
            picked = codes[0]
            for f in range(1, FEATURES):
                picked = jnp.where(chosen == f, codes[f], picked)
            return 2 * node_of + jnp.where(picked > cutoff, 1, 0)

        node4 = side(node, features3, bins3)
        leaf = side(node4, features4, bins4)
        leaf_ref[rows, :] = leaf
        leafrow_ref[rows, :] = leaf.astype(F32)
        for f in range(own_features):
            index = feat * own_features + f
            code = codes_ref[index // 8, pl.ds(step * 64 + index % 8, 8, stride=8), :]
            low_ref[f, rows, :] = (code & (LANES - 1)).astype(F32)
            key_ref[f, rows, :] = (node4 + NODES4 * (code >> 7)).astype(F32)
        weight = weight_ref[rows, :]
        label = label_ref[rows, :]
        rounded = weight.astype(BF16).astype(F32)
        wr_ref[rows, :] = rounded
        sr_ref[rows, :] = (weight * label).astype(BF16).astype(F32)
        rest = weight - rounded
        middle = rest.astype(BF16).astype(F32)
        low = rest - middle
        positive = label > 0.0
        for j, part in enumerate((rounded, middle, low)):
            stat_ref[pl.ds(step * 64 + j, 8, stride=8), :] = jnp.where(positive, part, 0.0)
            stat_ref[pl.ds(step * 64 + 3 + j, 8, stride=8), :] = jnp.where(positive, 0.0, part)
        for j in (6, 7):
            stat_ref[pl.ds(step * 64 + j, 8, stride=8), :] = jnp.zeros((8, LANES), F32)
        return carry

    def route_piece(c, carry):
        rows = pl.ds(pl.multiple_of(c * part, 8), part)
        pltpu.make_async_copy(codes_hbm.at[:, rows], codes_ref.at[:, rows], code_sem.at[c]).wait()
        first = c * (steps // CHUNKS)
        return lax.fori_loop(0, steps // CHUNKS, lambda i, x: route(first + i, x), carry, unroll=True)

    with jax.named_scope('route'):
        lax.fori_loop(0, CHUNKS, route_piece, 0)

    sub = lax.broadcasted_iota(jnp.int32, (16, LANES), 0).astype(F32)
    zero = jnp.zeros((16, LANES), BF16)
    one = jnp.ones((16, LANES), BF16)
    numbers = [(sub + 16 * i).astype(BF16) for i in range(8)]

    def spread(ref, *index):
        return jnp.broadcast_to(ref[index], (16, LANES)).astype(BF16)

    def dot_nt(a, b):
        return lax.dot_general(a, b, (((1,), (1,)), ((), ())), preferred_element_type=F32)

    def leaf_step(step, acc):
        left, right = [], []
        for i in range(8):
            t = step * 8 + i
            left.append(stat_ref[pl.ds(t * 8, 8), :].astype(BF16))
            at = spread(leafrow_ref, pl.ds(t, 1), slice(None))
            right.append(
                jnp.concatenate([jnp.where(at == numbers[k], one, zero) for k in range(2)], axis=0)
            )
        return acc + dot_nt(jnp.concatenate(left, axis=1), jnp.concatenate(right, axis=1))

    def send(source, target, sem, recv, peer):
        pltpu.make_async_remote_copy(
            src_ref=source, dst_ref=target, send_sem=sem, recv_sem=recv, device_id=peer, device_id_type=MESH
        ).start()

    def arrived(ref, sem):
        pltpu.make_async_copy(ref, ref, sem).wait()

    def leaf_scatter():
        leaf_sums = lax.fori_loop(0, steps, leaf_step, jnp.zeros((8, LEAVES), F32), unroll=5)
        leaf_a_ref[0, :, :] = jnp.zeros((8, LANES), F32)
        leaf_a_ref[0, :, :LEAVES] = leaf_sums
        for j in range(1, GROUP):
            send(leaf_a_ref.at[0], leaf_a_ref.at[j], leaf_send_sem.at[0], leaf_sem.at[0], in_group[j - 1])

    def leaf_exchange():
        with jax.named_scope('leafwait1'):
            arrived(leaf_a_ref.at[pl.ds(1, GROUP - 1)], leaf_sem.at[0])
        leaf_b_ref[0, :, :] = tree_sum([leaf_a_ref[j] for j in range(GROUP)])
        for j in range(1, GROUP):
            send(leaf_b_ref.at[0], leaf_b_ref.at[j], leaf_send_sem.at[1], leaf_sem.at[1], in_line[j - 1])

    def hist_step(f, step, acc):
        left, right = [], []
        for i in range(8):
            t = step * 8 + i
            key = spread(key_ref, f, pl.ds(t, 1), slice(None))
            low = spread(low_ref, f, pl.ds(t, 1), slice(None))
            wr = spread(wr_ref, pl.ds(t, 1), slice(None))
            sr = spread(sr_ref, pl.ds(t, 1), slice(None))
            blocks = []
            for hi in range(2):
                hit = key == numbers[hi]
                blocks += [jnp.where(hit, wr, zero), jnp.where(hit, sr, zero)]
            left.append(jnp.concatenate(blocks, axis=0))
            right.append(
                jnp.concatenate([jnp.where(low == numbers[k], one, zero) for k in range(8)], axis=0)
            )
        return acc + dot_nt(jnp.concatenate(right, axis=1), jnp.concatenate(left, axis=1))

    def compute(f):
        acc_ref[f, :, :] = lax.fori_loop(
            0, steps, functools.partial(hist_step, f), jnp.zeros((LANES, 64), F32), unroll=15
        ).T
        rs_ref[f, 0, :, :] = acc_ref[f, pl.ds(pl.multiple_of(group * 8, 8), 8), :]

    def scatter(f):
        for j in range(1, GROUP):
            rows = pl.ds(pl.multiple_of(flipped(group, j) * 8, 8), 8)
            send(acc_ref.at[f, rows], rs_ref.at[f, j], send_sem.at[f, 0], rs_sem.at[f], in_group[j - 1])

    def exchange(f):
        arrived(rs_ref.at[f, pl.ds(1, GROUP - 1)], rs_sem.at[f])
        ar_ref[f, 0, :, :] = tree_sum([rs_ref[f, j] for j in range(GROUP)])
        for j in range(1, GROUP):
            send(ar_ref.at[f, 0], ar_ref.at[f, j], send_sem.at[f, 1], ar_sem.at[f], in_line[j - 1])

    def gather(f):
        arrived(ar_ref.at[f, pl.ds(1, GROUP - 1)], ar_sem.at[f])
        mid_ref[f, :, :] = tree_sum([ar_ref[f, j] for j in range(GROUP)])
        rows = pl.ds(pl.multiple_of(group * 8, 8), 8)
        tot_ref[f, rows, :] = mid_ref[f, :, :]
        for j in range(1, GROUP):
            send(mid_ref.at[f], tot_ref.at[f, rows], send_sem.at[f, 2], ag_sem.at[f], in_group[j - 1])

    def grow_feature(f, carry):
        with jax.named_scope('compute'):
            compute(f)

        @pl.when(f == 1)
        def _():
            with jax.named_scope('barwait'):
                pl.semaphore_wait(barrier, 2 * (GROUP - 1))
            scatter(0)

        @pl.when(f >= 1)
        def _():
            scatter(f)

        return carry

    lax.fori_loop(0, own_features, grow_feature, 0)
    with jax.named_scope('exchange0'):
        exchange(0)
    with jax.named_scope('exchange1'):
        exchange(1)
    with jax.named_scope('leaf_scatter'):
        leaf_scatter()
    with jax.named_scope('exchange2'):
        exchange(2)
    with jax.named_scope('exchange3'):
        exchange(3)
    with jax.named_scope('leaf_exchange'):
        leaf_exchange()
    with jax.named_scope('gather0'):
        gather(0)
    with jax.named_scope('gather1'):
        gather(1)
    with jax.named_scope('gather2'):
        gather(2)
    with jax.named_scope('gather3'):
        gather(3)
    with jax.named_scope('leafwait2'):
        arrived(leaf_b_ref.at[pl.ds(1, GROUP - 1)], leaf_sem.at[1])
    leaf_mid_ref[...] = tree_sum([leaf_b_ref[j] for j in range(GROUP)])
    plus = leaf_mid_ref[0:1, :]
    minus = leaf_mid_ref[3:4, :]
    values = (plus - minus) / ((plus + minus) + 1.0)
    leaf_value_ref[...] = values[0, :LEAVES]
    all_plus = plus + (leaf_mid_ref[1:2, :] + leaf_mid_ref[2:3, :])
    all_minus = minus + (leaf_mid_ref[4:5, :] + leaf_mid_ref[5:6, :])
    grand = jnp.sum(all_plus * jnp.exp(-values) + all_minus * jnp.exp(values), axis=1, keepdims=True)
    scale = jnp.broadcast_to(total_rows / grand, (8, LANES))
    table = jnp.broadcast_to(values, (8, LANES))

    def update(step, carry):
        rows = pl.ds(step * 8, 8)
        stepped = jnp.take_along_axis(table, leaf_ref[rows, :], axis=1)
        new_pred_ref[rows, :] = pred_ref[rows, :] + stepped
        raw = weight_ref[rows, :] * jnp.exp(-label_ref[rows, :] * stepped)
        new_weight_ref[rows, :] = raw * scale
        return carry

    with jax.named_scope('update'):
        lax.fori_loop(0, steps, update, 0, unroll=5)

    everything = pl.ds(1, GROUP - 1)
    with jax.named_scope('sendwait'):
        for f in range(own_features):
            arrived(rs_ref.at[f, everything], send_sem.at[f, 0])
            arrived(ar_ref.at[f, everything], send_sem.at[f, 1])
        arrived(leaf_a_ref.at[everything], leaf_send_sem.at[0])
        arrived(leaf_b_ref.at[everything], leaf_send_sem.at[1])
    for f in range(own_features):
        with jax.named_scope('agwait'):
            arrived(tot_ref.at[f, pl.ds(0, 8 * (GROUP - 1))], ag_sem.at[f])
        for hi in range(2):
            lanes = slice(hi * LANES, (hi + 1) * LANES)
            base = hi * 2 * NODES4
            hist4_ref[f, :, lanes] = tot_ref[f, base : base + 2 * NODES4, :]
            even = tot_ref[f, pl.ds(base, 2 * NODES3, stride=2), :]
            odd = tot_ref[f, pl.ds(base + 1, 2 * NODES3, stride=2), :]
            hist3_ref[f, :, lanes] = even + odd
    with jax.named_scope('sendwait'):
        for f in range(own_features):
            arrived(tot_ref.at[f, pl.ds(0, 8 * (GROUP - 1))], send_sem.at[f, 2])


def store_kernel(*refs):
    count = len(refs) // 2
    sem = refs[-1]
    copies = [pltpu.make_async_copy(refs[i], refs[count + i], sem.at[i]) for i in range(count)]
    for copy in copies:
        copy.start()
    for copy in copies:
        copy.wait()


def on_device(bin_codes, node_ids, labels, weights, predictions, f3, b3, f4, b4):
    rows = node_ids.shape[0]
    tiles = rows // LANES
    total_rows = float(rows * lax.axis_size("rows"))
    own = FEATURES // lax.axis_size("feat")
    codes = bin_codes.reshape(FEATURES // 8, 8, tiles, LANES).transpose(0, 2, 1, 3)
    codes = codes.reshape(FEATURES // 8, tiles * 8, LANES)
    dense = [a.reshape(tiles, LANES) for a in (node_ids, labels, weights, predictions)]
    held = pl.BlockSpec(memory_space=pltpu.HBM)
    vmem = pl.BlockSpec(memory_space=pltpu.VMEM)
    outs = pl.pallas_call(
        functools.partial(kernel, total_rows, own),
        name="grow",
        in_specs=[held] * 9,
        out_specs=[vmem] * 5,
        out_shape=[
            jax.ShapeDtypeStruct((own, 2 * NODES3, BINS), F32),
            jax.ShapeDtypeStruct((own, 2 * NODES4, BINS), F32),
            jax.ShapeDtypeStruct((LEAVES,), F32),
            jax.ShapeDtypeStruct((tiles, LANES), F32),
            jax.ShapeDtypeStruct((tiles, LANES), F32),
        ],
        scratch_shapes=[
            pltpu.SMEM((NODES3,), jnp.int32),
            pltpu.SMEM((NODES3,), jnp.int32),
            pltpu.SMEM((NODES4,), jnp.int32),
            pltpu.SMEM((NODES4,), jnp.int32),
            pltpu.VMEM(codes.shape, jnp.int32),
            pltpu.VMEM((tiles, LANES), jnp.int32),
            pltpu.VMEM((tiles, LANES), F32),
            pltpu.VMEM((tiles, LANES), F32),
            pltpu.VMEM((tiles, LANES), F32),
            pltpu.VMEM((own, tiles, LANES), F32),
            pltpu.VMEM((own, tiles, LANES), F32),
            pltpu.VMEM((tiles, LANES), F32),
            pltpu.VMEM((tiles, LANES), F32),
            pltpu.VMEM((tiles, LANES), jnp.int32),
            pltpu.VMEM((tiles, LANES), F32),
            pltpu.VMEM((tiles * 8, LANES), F32),
            pltpu.VMEM((own, 64, LANES), F32),
            pltpu.VMEM((own, GROUP, 8, LANES), F32),
            pltpu.VMEM((own, 8, LANES), F32),
            pltpu.VMEM((own, GROUP, 8, LANES), F32),
            pltpu.VMEM((own, 64, LANES), F32),
            pltpu.VMEM((GROUP, 8, LANES), F32),
            pltpu.VMEM((GROUP, 8, LANES), F32),
            pltpu.VMEM((8, LANES), F32),
            pltpu.SemaphoreType.DMA((own, 3)),
            pltpu.SemaphoreType.DMA((own,)),
            pltpu.SemaphoreType.DMA((own,)),
            pltpu.SemaphoreType.DMA((own,)),
            pltpu.SemaphoreType.DMA((2,)),
            pltpu.SemaphoreType.DMA((2,)),
            pltpu.SemaphoreType.DMA((8,)),
            pltpu.SemaphoreType.DMA((CHUNKS,)),
        ],
        compiler_params=pltpu.CompilerParams(collective_id=0, has_side_effects=True, vmem_limit_bytes=16 << 20),
    )(*[pltpu.with_memory_space_constraint(a, pltpu.HBM) for a in (f3, b3, f4, b4, codes, *dense)])
    anywhere = pl.BlockSpec(memory_space=pl.ANY)
    hist3, hist4, leaf_values, new_pred, new_weight = pl.pallas_call(
        store_kernel,
        name="store",
        in_specs=[anywhere] * len(outs),
        out_specs=[anywhere] * len(outs),
        out_shape=[jax.ShapeDtypeStruct(a.shape, F32) for a in outs],
        scratch_shapes=[pltpu.SemaphoreType.DMA((len(outs),))],
        compiler_params=pltpu.CompilerParams(vmem_limit_bytes=1 << 20),
    )(*outs)
    return hist3, hist4, leaf_values, new_pred.reshape(rows), new_weight.reshape(rows)


def solution(mesh):
    placed = (P(None, "rows"), P("rows"), P("rows"), P("rows"), P("rows"), P(), P(), P(), P())
    return jax.shard_map(
        on_device,
        mesh=mesh,
        in_specs=placed,
        out_specs=(P("feat", None, None), P("feat", None, None), P(), P("rows"), P("rows")),
        check_vma=False,
    )
```

```python
import functools

import jax
import jax.numpy as jnp
from jax import lax
from jax.experimental import pallas as pl
from jax.experimental.pallas import tpu as pltpu
from jax.sharding import PartitionSpec as P

FEATURES = 16
BINS = 256
NODES3 = 8
NODES4 = 16
LEAVES = 32
LANES = 128
CHUNKS = 3
GROUP = 8
GROUP_ORDER = (5, 4, 7, 6, 3, 2, 1)
LINE_ORDER = (4, 5, 3, 7, 6, 2, 1)
MESH = pl.DeviceIdType.MESH
F32 = jnp.float32
BF16 = jnp.bfloat16


def flipped(index, mask):
    out = index
    for bit in (1, 2, 4):
        if mask & bit:
            out = out + bit * (1 - 2 * ((index // bit) % 2))
    return out


def tree_sum(parts):
    while len(parts) > 1:
        parts = [a + b for a, b in zip(parts[::2], parts[1::2])]
    return parts[0]


def kernel(
    total_rows,
    own_features,
    f3_hbm,
    b3_hbm,
    f4_hbm,
    b4_hbm,
    codes_hbm,
    node_hbm,
    label_hbm,
    weight_hbm,
    pred_hbm,
    hist3_ref,
    hist4_ref,
    leaf_value_ref,
    new_pred_ref,
    new_weight_ref,
    f3_ref,
    b3_ref,
    f4_ref,
    b4_ref,
    codes_ref,
    node_ref,
    label_ref,
    weight_ref,
    pred_ref,
    key_ref,
    low_ref,
    wr_ref,
    sr_ref,
    node4_ref,
    leaf_ref,
    leafrow_ref,
    stat_ref,
    acc_ref,
    rs_ref,
    mid_ref,
    ar_ref,
    tot_ref,
    leaf_a_ref,
    leaf_b_ref,
    leaf_mid_ref,
    send_sem,
    rs_sem,
    ar_sem,
    ag_sem,
    leaf_sem,
    in_sem,
    code_sem,
):
    tiles = node_hbm.shape[0]
    steps = tiles // 8
    row = lax.axis_index("rows")
    feat = lax.axis_index("feat")
    group = row % GROUP
    plane = row // GROUP
    in_group = [(plane * GROUP + flipped(group, j), feat) for j in range(1, GROUP)]
    in_line = [(flipped(plane, j) * GROUP + group, feat) for j in range(1, GROUP)]

    def fetch(source, target, sem):
        copy = pltpu.make_async_copy(source, target, sem)
        copy.start()
        return copy

    part = tiles * 8 // CHUNKS
    for a, b in ((node_hbm, node_ref), (weight_hbm, weight_ref), (label_hbm, label_ref)):
        fetch(a, b, in_sem.at[4])
    tables = ((f3_hbm, f3_ref), (b3_hbm, b3_ref), (f4_hbm, f4_ref), (b4_hbm, b4_ref))
    ready = [fetch(a, b, in_sem.at[i]) for i, (a, b) in enumerate(tables)]
    for c in range(CHUNKS):
        rows = pl.ds(c * part, part)
        fetch(codes_hbm.at[:, rows], codes_ref.at[:, rows], code_sem.at[c])
    pred_ready = fetch(pred_hbm, pred_ref, in_sem.at[5])

    barrier = pltpu.get_barrier_semaphore()
    with jax.named_scope('signal'):
        for peer in in_group + in_line:
            pl.semaphore_signal(barrier, inc=1, device_id=peer, device_id_type=MESH)

    with jax.named_scope('inwait'):
        for copy in ready:
            copy.wait()
        whole = stat_ref.at[pl.ds(0, 3 * tiles)]
        pltpu.make_async_copy(whole, whole, in_sem.at[4]).wait()

    features3 = [f3_ref[i] for i in range(NODES3)]
    bins3 = [b3_ref[i] for i in range(NODES3)]
    features4 = [f4_ref[i] for i in range(NODES4)]
    bins4 = [b4_ref[i] for i in range(NODES4)]

    def lookup(where_of, tables):
        outs = [jnp.full((8, LANES), table[0], jnp.int32) for table in tables]
        for i in range(1, len(tables[0])):
            hit = where_of == i
            outs = [jnp.where(hit, table[i], out) for table, out in zip(tables, outs)]
        return outs

    def side(step, node_of, features, bins):
        codes = [codes_ref[f // 8, pl.ds(step * 64 + f % 8, 8, stride=8), :] for f in range(FEATURES)]
        chosen, cutoff = lookup(node_of, [features, bins])
        picked = codes[0]
        for f in range(1, FEATURES):
            picked = jnp.where(chosen == f, codes[f], picked)
        return 2 * node_of + jnp.where(picked > cutoff, 1, 0)

    def route(step, carry):
        rows = pl.ds(step * 8, 8)
        node4 = side(step, node_ref[rows, :], features3, bins3)
        node4_ref[rows, :] = node4
        for f in range(own_features):
            index = feat * own_features + f
            code = codes_ref[index // 8, pl.ds(step * 64 + index % 8, 8, stride=8), :]
            low_ref[f, rows, :] = (code & (LANES - 1)).astype(F32)
            key_ref[f, rows, :] = (node4 + NODES4 * (code >> 7)).astype(F32)
        weight = weight_ref[rows, :]
        wr_ref[rows, :] = weight.astype(BF16).astype(F32)
        sr_ref[rows, :] = (weight * label_ref[rows, :]).astype(BF16).astype(F32)
        return carry

    def leaf_route(step, carry):
        rows = pl.ds(step * 8, 8)
        leaf = side(step, node4_ref[rows, :], features4, bins4)
        leaf_ref[rows, :] = leaf
        leafrow_ref[rows, :] = leaf.astype(F32)
        weight = weight_ref[rows, :]
        positive = label_ref[rows, :] > 0.0
        rounded = wr_ref[rows, :]
        rest = weight - rounded
        middle = rest.astype(BF16).astype(F32)
        low = rest - middle
        for j, term in enumerate((rounded, middle, low)):
            stat_ref[pl.ds(step * 64 + j, 8, stride=8), :] = jnp.where(positive, term, 0.0)
            stat_ref[pl.ds(step * 64 + 3 + j, 8, stride=8), :] = jnp.where(positive, 0.0, term)
        for j in (6, 7):
            stat_ref[pl.ds(step * 64 + j, 8, stride=8), :] = jnp.zeros((8, LANES), F32)
        return carry

    def route_piece(c, carry):
        rows = pl.ds(pl.multiple_of(c * part, 8), part)
        pltpu.make_async_copy(codes_hbm.at[:, rows], codes_ref.at[:, rows], code_sem.at[c]).wait()
        first = c * (steps // CHUNKS)
        return lax.fori_loop(0, steps // CHUNKS, lambda i, x: route(first + i, x), carry, unroll=True)

    with jax.named_scope('route'):
        lax.fori_loop(0, CHUNKS, route_piece, 0)

    sub = lax.broadcasted_iota(jnp.int32, (16, LANES), 0).astype(F32)
    zero = jnp.zeros((16, LANES), BF16)
    one = jnp.ones((16, LANES), BF16)
    numbers = [(sub + 16 * i).astype(BF16) for i in range(8)]

    def spread(ref, *index):
        return jnp.broadcast_to(ref[index], (16, LANES)).astype(BF16)

    def dot_nt(a, b):
        return lax.dot_general(a, b, (((1,), (1,)), ((), ())), preferred_element_type=F32)

    def leaf_step(step, acc):
        left, right = [], []
        for i in range(8):
            t = step * 8 + i
            left.append(stat_ref[pl.ds(t * 8, 8), :].astype(BF16))
            at = spread(leafrow_ref, pl.ds(t, 1), slice(None))
            right.append(
                jnp.concatenate([jnp.where(at == numbers[k], one, zero) for k in range(2)], axis=0)
            )
        return acc + dot_nt(jnp.concatenate(left, axis=1), jnp.concatenate(right, axis=1))

    def send(source, target, recv, peer):
        pltpu.make_async_remote_copy(
            src_ref=source, dst_ref=target, send_sem=send_sem, recv_sem=recv, device_id=peer, device_id_type=MESH
        ).start()

    def arrived(ref, sem):
        pltpu.make_async_copy(ref, ref, sem).wait()

    others = pl.ds(1, GROUP - 1)
    own_rows = pl.ds(pl.multiple_of(group * 8, 8), 8)

    def leaf_scatter():
        lax.fori_loop(0, steps, leaf_route, 0, unroll=3)
        leaf_sums = lax.fori_loop(0, steps, leaf_step, jnp.zeros((8, LEAVES), F32), unroll=5)
        leaf_a_ref[0, :, :] = jnp.zeros((8, LANES), F32)
        leaf_a_ref[0, :, :LEAVES] = leaf_sums
        for j in GROUP_ORDER:
            send(leaf_a_ref.at[0], leaf_a_ref.at[j], leaf_sem.at[0], in_group[j - 1])

    def leaf_exchange():
        with jax.named_scope('leafwait1'):
            arrived(leaf_a_ref.at[others], leaf_sem.at[0])
        leaf_b_ref[0, :, :] = tree_sum([leaf_a_ref[j] for j in range(GROUP)])
        for j in LINE_ORDER:
            send(leaf_b_ref.at[0], leaf_b_ref.at[j], leaf_sem.at[1], in_line[j - 1])

    def hist_step(f, step, acc):
        left, right = [], []
        for i in range(8):
            t = step * 8 + i
            key = spread(key_ref, f, pl.ds(t, 1), slice(None))
            low = spread(low_ref, f, pl.ds(t, 1), slice(None))
            wr = spread(wr_ref, pl.ds(t, 1), slice(None))
            sr = spread(sr_ref, pl.ds(t, 1), slice(None))
            blocks = []
            for hi in range(2):
                hit = key == numbers[hi]
                blocks += [jnp.where(hit, wr, zero), jnp.where(hit, sr, zero)]
            left.append(jnp.concatenate(blocks, axis=0))
            right.append(
                jnp.concatenate([jnp.where(low == numbers[k], one, zero) for k in range(8)], axis=0)
            )
        return acc + dot_nt(jnp.concatenate(right, axis=1), jnp.concatenate(left, axis=1))

    def compute(f):
        acc_ref[f, :, :] = lax.fori_loop(
            0, steps, functools.partial(hist_step, f), jnp.zeros((LANES, 64), F32), unroll=15
        ).T

    def scatter(c, first, count):
        some = pl.ds(first, count)
        for j in GROUP_ORDER:
            rows = pl.ds(pl.multiple_of(flipped(group, j) * 8, 8), 8)
            send(acc_ref.at[some, rows], rs_ref.at[j, some], rs_sem.at[c], in_group[j - 1])
        rs_ref[0, some, :, :] = acc_ref[some, own_rows, :]

    def exchange(c, first, count):
        some = pl.ds(first, count)
        with jax.named_scope('rswait'):
            arrived(rs_ref.at[others, some], rs_sem.at[c])
        ar_ref[0, some, :, :] = tree_sum([rs_ref[j, some] for j in range(GROUP)])
        for j in LINE_ORDER:
            send(ar_ref.at[0, some], ar_ref.at[j, some], ar_sem.at[c], in_line[j - 1])

    def gather(c, first, count):
        some = pl.ds(first, count)
        with jax.named_scope('arwait'):
            arrived(ar_ref.at[others, some], ar_sem.at[c])
        mid_ref[some, :, :] = tree_sum([ar_ref[j, some] for j in range(GROUP)])
        for j in GROUP_ORDER:
            send(mid_ref.at[some], tot_ref.at[some, own_rows], ag_sem.at[c], in_group[j - 1])
        tot_ref[some, own_rows, :] = mid_ref[some, :, :]

    with jax.named_scope('compute'):
        compute(0)
        compute(1)
    with jax.named_scope('barwait'):
        pl.semaphore_wait(barrier, 2 * (GROUP - 1))
    scatter(0, 0, 2)

    def grow_one(f, carry):
        with jax.named_scope('compute'):
            compute(f)
        scatter(f - 1, f, 1)
        return carry

    lax.fori_loop(2, own_features, grow_one, 0)
    batches = ((0, 0, 2), (1, 2, 1), (2, 3, 1))
    with jax.named_scope('leaf_scatter'):
        leaf_scatter()
    for batch in batches:
        exchange(*batch)
    leaf_exchange()
    for batch in batches:
        gather(*batch)
    with jax.named_scope('leafwait2'):
        arrived(leaf_b_ref.at[others], leaf_sem.at[1])
    leaf_mid_ref[...] = tree_sum([leaf_b_ref[j] for j in range(GROUP)])
    plus = leaf_mid_ref[0:1, :]
    minus = leaf_mid_ref[3:4, :]
    values = (plus - minus) / ((plus + minus) + 1.0)
    leaf_value_ref[...] = values[0, :LEAVES]
    all_plus = plus + (leaf_mid_ref[1:2, :] + leaf_mid_ref[2:3, :])
    all_minus = minus + (leaf_mid_ref[4:5, :] + leaf_mid_ref[5:6, :])
    grand = jnp.sum(all_plus * jnp.exp(-values) + all_minus * jnp.exp(values), axis=1, keepdims=True)
    scale = jnp.broadcast_to(total_rows / grand, (8, LANES))
    table = jnp.broadcast_to(values, (8, LANES))

    def update(step, carry):
        rows = pl.ds(step * 8, 8)
        stepped = jnp.take_along_axis(table, leaf_ref[rows, :], axis=1)
        new_pred_ref[rows, :] = pred_ref[rows, :] + stepped
        raw = weight_ref[rows, :] * jnp.exp(-label_ref[rows, :] * stepped)
        new_weight_ref[rows, :] = raw * scale
        return carry

    pred_ready.wait()
    with jax.named_scope('update'):
        lax.fori_loop(0, steps, update, 0, unroll=5)

    for c, first, count in batches:
        with jax.named_scope('agwait'):
            arrived(tot_ref.at[pl.ds(first, count), pl.ds(0, 8 * (GROUP - 1))], ag_sem.at[c])
        for f in range(first, first + count):
            for hi in range(2):
                lanes = slice(hi * LANES, (hi + 1) * LANES)
                base = hi * 2 * NODES4
                hist4_ref[f, :, lanes] = tot_ref[f, base : base + 2 * NODES4, :]
                even = tot_ref[f, pl.ds(base, 2 * NODES3, stride=2), :]
                odd = tot_ref[f, pl.ds(base + 1, 2 * NODES3, stride=2), :]
                hist3_ref[f, :, lanes] = even + odd
    sent = (3 * own_features + 2) * (GROUP - 1) * 8
    with jax.named_scope('sendwait'):
        arrived(codes_ref.at[0, pl.ds(0, sent)], send_sem)


def store_kernel(*refs):
    count = len(refs) // 2
    sem = refs[-1]
    copies = [pltpu.make_async_copy(refs[i], refs[count + i], sem.at[i]) for i in range(count)]
    for copy in copies:
        copy.start()
    for copy in copies:
        copy.wait()


def on_device(bin_codes, node_ids, labels, weights, predictions, f3, b3, f4, b4):
    rows = node_ids.shape[0]
    tiles = rows // LANES
    total_rows = float(rows * lax.axis_size("rows"))
    own = FEATURES // lax.axis_size("feat")
    codes = bin_codes.reshape(FEATURES // 8, 8, tiles, LANES).transpose(0, 2, 1, 3)
    codes = codes.reshape(FEATURES // 8, tiles * 8, LANES)
    dense = [a.reshape(tiles, LANES) for a in (node_ids, labels, weights, predictions)]
    held = pl.BlockSpec(memory_space=pltpu.HBM)
    vmem = pl.BlockSpec(memory_space=pltpu.VMEM)
    outs = pl.pallas_call(
        functools.partial(kernel, total_rows, own),
        name="grow",
        in_specs=[held] * 9,
        out_specs=[vmem] * 5,
        out_shape=[
            jax.ShapeDtypeStruct((own, 2 * NODES3, BINS), F32),
            jax.ShapeDtypeStruct((own, 2 * NODES4, BINS), F32),
            jax.ShapeDtypeStruct((LEAVES,), F32),
            jax.ShapeDtypeStruct((tiles, LANES), F32),
            jax.ShapeDtypeStruct((tiles, LANES), F32),
        ],
        scratch_shapes=[
            pltpu.SMEM((NODES3,), jnp.int32),
            pltpu.SMEM((NODES3,), jnp.int32),
            pltpu.SMEM((NODES4,), jnp.int32),
            pltpu.SMEM((NODES4,), jnp.int32),
            pltpu.VMEM(codes.shape, jnp.int32),
            pltpu.VMEM((tiles, LANES), jnp.int32),
            pltpu.VMEM((tiles, LANES), F32),
            pltpu.VMEM((tiles, LANES), F32),
            pltpu.VMEM((tiles, LANES), F32),
            pltpu.VMEM((own, tiles, LANES), F32),
            pltpu.VMEM((own, tiles, LANES), F32),
            pltpu.VMEM((tiles, LANES), F32),
            pltpu.VMEM((tiles, LANES), F32),
            pltpu.VMEM((tiles, LANES), jnp.int32),
            pltpu.VMEM((tiles, LANES), jnp.int32),
            pltpu.VMEM((tiles, LANES), F32),
            pltpu.VMEM((tiles * 8, LANES), F32),
            pltpu.VMEM((own, 64, LANES), F32),
            pltpu.VMEM((GROUP, own, 8, LANES), F32),
            pltpu.VMEM((own, 8, LANES), F32),
            pltpu.VMEM((GROUP, own, 8, LANES), F32),
            pltpu.VMEM((own, 64, LANES), F32),
            pltpu.VMEM((GROUP, 8, LANES), F32),
            pltpu.VMEM((GROUP, 8, LANES), F32),
            pltpu.VMEM((8, LANES), F32),
            pltpu.SemaphoreType.DMA(()),
            pltpu.SemaphoreType.DMA((3,)),
            pltpu.SemaphoreType.DMA((3,)),
            pltpu.SemaphoreType.DMA((3,)),
            pltpu.SemaphoreType.DMA((2,)),
            pltpu.SemaphoreType.DMA((6,)),
            pltpu.SemaphoreType.DMA((CHUNKS,)),
        ],
        compiler_params=pltpu.CompilerParams(collective_id=0, has_side_effects=True, vmem_limit_bytes=16 << 20),
    )(*[pltpu.with_memory_space_constraint(a, pltpu.HBM) for a in (f3, b3, f4, b4, codes, *dense)])
    anywhere = pl.BlockSpec(memory_space=pl.ANY)
    hist3, hist4, leaf_values, new_pred, new_weight = pl.pallas_call(
        store_kernel,
        name="store",
        in_specs=[anywhere] * len(outs),
        out_specs=[anywhere] * len(outs),
        out_shape=[jax.ShapeDtypeStruct(a.shape, F32) for a in outs],
        scratch_shapes=[pltpu.SemaphoreType.DMA((len(outs),))],
        compiler_params=pltpu.CompilerParams(vmem_limit_bytes=1 << 20),
    )(*outs)
    return hist3, hist4, leaf_values, new_pred.reshape(rows), new_weight.reshape(rows)


def solution(mesh):
    placed = (P(None, "rows"), P("rows"), P("rows"), P("rows"), P("rows"), P(), P(), P(), P())
    return jax.shard_map(
        on_device,
        mesh=mesh,
        in_specs=placed,
        out_specs=(P("feat", None, None), P("feat", None, None), P(), P("rows"), P("rows")),
        check_vma=False,
    )
```

```python
import functools

import jax
import jax.numpy as jnp
from jax import lax
from jax.experimental import pallas as pl
from jax.experimental.pallas import tpu as pltpu
from jax.sharding import PartitionSpec as P

FEATURES = 16
BINS = 256
NODES3 = 8
NODES4 = 16
LEAVES = 32
LANES = 128
CHUNKS = 3
GROUP = 8
GROUP_ORDER = (5, 4, 7, 6, 3, 2, 1)
LINE_ORDER = (4, 5, 3, 7, 6, 2, 1)
MESH = pl.DeviceIdType.MESH
F32 = jnp.float32
BF16 = jnp.bfloat16


def flipped(index, mask):
    out = index
    for bit in (1, 2, 4):
        if mask & bit:
            out = out + bit * (1 - 2 * ((index // bit) % 2))
    return out


def tree_sum(parts):
    while len(parts) > 1:
        parts = [a + b for a, b in zip(parts[::2], parts[1::2])]
    return parts[0]


def kernel(
    total_rows,
    own_features,
    f3_hbm,
    b3_hbm,
    f4_hbm,
    b4_hbm,
    codes_hbm,
    node_hbm,
    label_hbm,
    weight_hbm,
    pred_hbm,
    hist3_ref,
    hist4_ref,
    leaf_value_ref,
    new_pred_ref,
    new_weight_ref,
    f3_ref,
    b3_ref,
    f4_ref,
    b4_ref,
    codes_ref,
    node_ref,
    label_ref,
    weight_ref,
    pred_ref,
    key_ref,
    low_ref,
    wr_ref,
    sr_ref,
    node4_ref,
    leaf_ref,
    leafrow_ref,
    stat_ref,
    acc_ref,
    rs_ref,
    mid_ref,
    ar_ref,
    tot_ref,
    rs_last_ref,
    ar_last_ref,
    mid_last_ref,
    leaf_a_ref,
    leaf_b_ref,
    leaf_mid_ref,
    send_sem,
    rs_sem,
    ar_sem,
    ag_sem,
    leaf_sem,
    in_sem,
    code_sem,
):
    tiles = node_hbm.shape[0]
    steps = tiles // 8
    row = lax.axis_index("rows")
    feat = lax.axis_index("feat")
    group = row % GROUP
    plane = row // GROUP
    in_group = [(plane * GROUP + flipped(group, j), feat) for j in range(1, GROUP)]
    in_line = [(flipped(plane, j) * GROUP + group, feat) for j in range(1, GROUP)]

    def fetch(source, target, sem):
        copy = pltpu.make_async_copy(source, target, sem)
        copy.start()
        return copy

    part = tiles * 8 // CHUNKS
    def fetch_codes(c):
        rows = pl.ds(c * part, part)
        fetch(codes_hbm.at[:, rows], codes_ref.at[:, rows], code_sem.at[c])

    node_ready = fetch(node_hbm, node_ref, in_sem.at[6])
    fetch_codes(0)
    tables = ((f3_hbm, f3_ref), (b3_hbm, b3_ref), (f4_hbm, f4_ref), (b4_hbm, b4_ref))
    ready = [fetch(a, b, in_sem.at[i]) for i, (a, b) in enumerate(tables)]
    for c in range(1, CHUNKS):
        fetch_codes(c)
    for a, b in ((weight_hbm, weight_ref), (label_hbm, label_ref)):
        fetch(a, b, in_sem.at[4])
    pred_ready = fetch(pred_hbm, pred_ref, in_sem.at[5])

    barrier = pltpu.get_barrier_semaphore()
    with jax.named_scope('signal'):
        for peer in in_group + in_line:
            pl.semaphore_signal(barrier, inc=1, device_id=peer, device_id_type=MESH)

    with jax.named_scope('inwait'):
        for copy in ready:
            copy.wait()
        node_ready.wait()

    features3 = [f3_ref[i] for i in range(NODES3)]
    bins3 = [b3_ref[i] for i in range(NODES3)]
    features4 = [f4_ref[i] for i in range(NODES4)]
    bins4 = [b4_ref[i] for i in range(NODES4)]

    def lookup(where_of, tables):
        outs = [jnp.full((8, LANES), table[0], jnp.int32) for table in tables]
        for i in range(1, len(tables[0])):
            hit = where_of == i
            outs = [jnp.where(hit, table[i], out) for table, out in zip(tables, outs)]
        return outs

    def side(step, node_of, features, bins):
        codes = [codes_ref[f // 8, pl.ds(step * 64 + f % 8, 8, stride=8), :] for f in range(FEATURES)]
        chosen, cutoff = lookup(node_of, [features, bins])
        picked = codes[0]
        for f in range(1, FEATURES):
            picked = jnp.where(chosen == f, codes[f], picked)
        return 2 * node_of + jnp.where(picked > cutoff, 1, 0)

    def route(step, carry):
        rows = pl.ds(step * 8, 8)
        node4 = side(step, node_ref[rows, :], features3, bins3)
        node4_ref[rows, :] = node4
        for f in range(own_features):
            index = feat * own_features + f
            code = codes_ref[index // 8, pl.ds(step * 64 + index % 8, 8, stride=8), :]
            low_ref[f, rows, :] = (code & (LANES - 1)).astype(F32)
            key_ref[f, rows, :] = (node4 + NODES4 * (code >> 7)).astype(F32)
        return carry

    def rounding(step, carry):
        rows = pl.ds(step * 8, 8)
        weight = weight_ref[rows, :]
        wr_ref[rows, :] = weight.astype(BF16).astype(F32)
        sr_ref[rows, :] = (weight * label_ref[rows, :]).astype(BF16).astype(F32)
        return carry

    def leaf_route(step, carry):
        rows = pl.ds(step * 8, 8)
        leaf = side(step, node4_ref[rows, :], features4, bins4)
        leaf_ref[rows, :] = leaf
        leafrow_ref[rows, :] = leaf.astype(F32)
        weight = weight_ref[rows, :]
        positive = label_ref[rows, :] > 0.0
        rounded = wr_ref[rows, :]
        rest = weight - rounded
        middle = rest.astype(BF16).astype(F32)
        low = rest - middle
        for j, term in enumerate((rounded, middle, low)):
            stat_ref[pl.ds(step * 64 + j, 8, stride=8), :] = jnp.where(positive, term, 0.0)
            stat_ref[pl.ds(step * 64 + 3 + j, 8, stride=8), :] = jnp.where(positive, 0.0, term)
        for j in (6, 7):
            stat_ref[pl.ds(step * 64 + j, 8, stride=8), :] = jnp.zeros((8, LANES), F32)
        return carry

    def route_piece(c, carry):
        rows = pl.ds(pl.multiple_of(c * part, 8), part)
        pltpu.make_async_copy(codes_hbm.at[:, rows], codes_ref.at[:, rows], code_sem.at[c]).wait()
        first = c * (steps // CHUNKS)
        return lax.fori_loop(0, steps // CHUNKS, lambda i, x: route(first + i, x), carry, unroll=True)

    with jax.named_scope('route'):
        lax.fori_loop(0, CHUNKS, route_piece, 0)
        whole = stat_ref.at[pl.ds(0, 2 * tiles)]
        pltpu.make_async_copy(whole, whole, in_sem.at[4]).wait()
        lax.fori_loop(0, steps, rounding, 0, unroll=True)

    sub = lax.broadcasted_iota(jnp.int32, (16, LANES), 0).astype(F32)
    zero = jnp.zeros((16, LANES), BF16)
    one = jnp.ones((16, LANES), BF16)
    numbers = [(sub + 16 * i).astype(BF16) for i in range(8)]

    def spread(ref, *index):
        return jnp.broadcast_to(ref[index], (16, LANES)).astype(BF16)

    def dot_nt(a, b):
        return lax.dot_general(a, b, (((1,), (1,)), ((), ())), preferred_element_type=F32)

    def leaf_step(step, acc):
        left, right = [], []
        for i in range(8):
            t = step * 8 + i
            left.append(stat_ref[pl.ds(t * 8, 8), :].astype(BF16))
            at = spread(leafrow_ref, pl.ds(t, 1), slice(None))
            right.append(
                jnp.concatenate([jnp.where(at == numbers[k], one, zero) for k in range(2)], axis=0)
            )
        return acc + dot_nt(jnp.concatenate(left, axis=1), jnp.concatenate(right, axis=1))

    def send(source, target, recv, peer):
        pltpu.make_async_remote_copy(
            src_ref=source, dst_ref=target, send_sem=send_sem, recv_sem=recv, device_id=peer, device_id_type=MESH
        ).start()

    def arrived(ref, sem):
        pltpu.make_async_copy(ref, ref, sem).wait()

    others = pl.ds(1, GROUP - 1)

    def tile_of(index):
        return index // 4, pl.ds(pl.multiple_of((index % 4) * 8, 8), 8)

    own_high, own_rows = tile_of(group)

    def leaf_scatter():
        lax.fori_loop(0, steps, leaf_route, 0, unroll=3)
        leaf_sums = lax.fori_loop(0, steps, leaf_step, jnp.zeros((8, LEAVES), F32), unroll=5)
        leaf_a_ref[0, :, :] = jnp.zeros((8, LANES), F32)
        leaf_a_ref[0, :, :LEAVES] = leaf_sums
        for j in GROUP_ORDER:
            send(leaf_a_ref.at[0], leaf_a_ref.at[j], leaf_sem.at[0], in_group[j - 1])

    def leaf_exchange():
        with jax.named_scope('leafwait1'):
            arrived(leaf_a_ref.at[others], leaf_sem.at[0])
        leaf_b_ref[0, :, :] = tree_sum([leaf_a_ref[j] for j in range(GROUP)])
        for j in LINE_ORDER:
            send(leaf_b_ref.at[0], leaf_b_ref.at[j], leaf_sem.at[1], in_line[j - 1])

    def hist_step(f, step, acc):
        left, right = [], []
        for i in range(8):
            t = step * 8 + i
            key = spread(key_ref, f, pl.ds(t, 1), slice(None))
            low = spread(low_ref, f, pl.ds(t, 1), slice(None))
            wr = spread(wr_ref, pl.ds(t, 1), slice(None))
            sr = spread(sr_ref, pl.ds(t, 1), slice(None))
            blocks = []
            for hi in range(2):
                hit = key == numbers[hi]
                blocks += [jnp.where(hit, wr, zero), jnp.where(hit, sr, zero)]
            left.append(jnp.concatenate(blocks, axis=0))
            right.append(
                jnp.concatenate([jnp.where(low == numbers[k], one, zero) for k in range(8)], axis=0)
            )
        return acc + dot_nt(jnp.concatenate(right, axis=1), jnp.concatenate(left, axis=1))

    def compute(f):
        acc = lax.fori_loop(
            0, steps, functools.partial(hist_step, f), jnp.zeros((LANES, 64), F32), unroll=15
        ).T
        acc_ref[f, 0, :, :] = acc[: 2 * NODES4]
        acc_ref[f, 1, :, :] = acc[2 * NODES4 :]

    def scatter(c, first, count):
        some = pl.ds(first, count)
        for j in GROUP_ORDER:
            high, rows = tile_of(flipped(group, j))
            send(acc_ref.at[some, high, rows], rs_ref.at[j, some], rs_sem.at[c], in_group[j - 1])
        rs_ref[0, some, :, :] = acc_ref[some, own_high, own_rows, :]

    def exchange(c, first, count):
        some = pl.ds(first, count)
        with jax.named_scope('rswait'):
            arrived(rs_ref.at[others, some], rs_sem.at[c])
        ar_ref[0, some, :, :] = tree_sum([rs_ref[j, some] for j in range(GROUP)])
        for j in LINE_ORDER:
            send(ar_ref.at[0, some], ar_ref.at[j, some], ar_sem.at[c], in_line[j - 1])

    def gather(c, first, count):
        some = pl.ds(first, count)
        with jax.named_scope('arwait'):
            arrived(ar_ref.at[others, some], ar_sem.at[c])
        mid_ref[some, :, :] = tree_sum([ar_ref[j, some] for j in range(GROUP)])
        for j in GROUP_ORDER:
            send(mid_ref.at[some], tot_ref.at[some, own_high, own_rows], ag_sem.at[c], in_group[j - 1])
        tot_ref[some, own_high, own_rows, :] = mid_ref[some, :, :]

    last = own_features - 1

    def scatter_last():
        for j in GROUP_ORDER:
            _, rows = tile_of(flipped(group, j))
            send(acc_ref.at[last, :, rows], rs_last_ref.at[j], rs_sem.at[2], in_group[j - 1])
        rs_last_ref[0, :, :, :] = acc_ref[last, :, own_rows, :]

    def exchange_last():
        with jax.named_scope('rswait'):
            arrived(rs_last_ref.at[others], rs_sem.at[2])
        ar_last_ref[0, :, :, :] = tree_sum([rs_last_ref[j] for j in range(GROUP)])
        for j in LINE_ORDER:
            send(ar_last_ref.at[0], ar_last_ref.at[j], ar_sem.at[2], in_line[j - 1])

    def gather_last():
        core = group % 2
        near = [flipped(group, j) + core * (flipped(group, j + 4) - flipped(group, j)) for j in (3, 2)]
        near.append(flipped(group, 1))
        with jax.named_scope('arwait'):
            arrived(ar_last_ref.at[others], ar_sem.at[2])
        mid_last_ref[...] = tree_sum([ar_last_ref[j] for j in range(GROUP)])
        for peer in near:
            send(mid_last_ref, tot_ref.at[last, :, own_rows], ag_sem.at[2], (plane * GROUP + peer, feat))
        tot_ref[last, :, own_rows, :] = mid_last_ref[...]

    with jax.named_scope('compute'):
        compute(0)
        compute(1)
    with jax.named_scope('barwait'):
        pl.semaphore_wait(barrier, 2 * (GROUP - 1))
    scatter(0, 0, 2)

    def grow_one(f, carry):
        with jax.named_scope('compute'):
            compute(f)

        @pl.when(f < last)
        def _():
            scatter(1, 2, 1)

        @pl.when(f == last)
        def _():
            scatter_last()

        return carry

    lax.fori_loop(2, own_features, grow_one, 0)
    batches = ((0, 0, 2), (1, 2, 1))
    exchange(*batches[0])
    with jax.named_scope('leaf_scatter'):
        leaf_scatter()
    exchange(*batches[1])
    exchange_last()
    leaf_exchange()
    for batch in batches:
        gather(*batch)
    gather_last()
    with jax.named_scope('leafwait2'):
        arrived(leaf_b_ref.at[others], leaf_sem.at[1])
    leaf_mid_ref[...] = tree_sum([leaf_b_ref[j] for j in range(GROUP)])
    plus = leaf_mid_ref[0:1, :]
    minus = leaf_mid_ref[3:4, :]
    values = (plus - minus) / ((plus + minus) + 1.0)
    leaf_value_ref[...] = values[0, :LEAVES]
    all_plus = plus + (leaf_mid_ref[1:2, :] + leaf_mid_ref[2:3, :])
    all_minus = minus + (leaf_mid_ref[4:5, :] + leaf_mid_ref[5:6, :])
    grand = jnp.sum(all_plus * jnp.exp(-values) + all_minus * jnp.exp(values), axis=1, keepdims=True)
    scale = jnp.broadcast_to(total_rows / grand, (8, LANES))
    table = jnp.broadcast_to(values, (8, LANES))

    def update(step, carry):
        rows = pl.ds(step * 8, 8)
        stepped = jnp.take_along_axis(table, leaf_ref[rows, :], axis=1)
        new_pred_ref[rows, :] = pred_ref[rows, :] + stepped
        raw = weight_ref[rows, :] * jnp.exp(-label_ref[rows, :] * stepped)
        new_weight_ref[rows, :] = raw * scale
        return carry

    pred_ready.wait()
    with jax.named_scope('update'):
        lax.fori_loop(0, steps, update, 0, unroll=5)

    def store(f):
        for hi in range(2):
            lanes = slice(hi * LANES, (hi + 1) * LANES)
            hist4_ref[f, :, lanes] = tot_ref[f, hi]
            even = tot_ref[f, hi, pl.ds(0, 2 * NODES3, stride=2), :]
            odd = tot_ref[f, hi, pl.ds(1, 2 * NODES3, stride=2), :]
            hist3_ref[f, :, lanes] = even + odd

    for c, first, count in batches:
        with jax.named_scope('agwait'):
            whole = stat_ref.at[pl.ds(0, count * 8 * (GROUP - 1))]
            arrived(whole, ag_sem.at[c])
        for f in range(first, first + count):
            store(f)
    with jax.named_scope('agwait'):
        arrived(tot_ref.at[last, :, pl.ds(0, 24)], ag_sem.at[2])
    store(last)
    tiles_sent = (3 * last + 2) * (GROUP - 1) + 2 * (2 * (GROUP - 1) + 3)
    sent = tiles_sent * 8
    with jax.named_scope('sendwait'):
        arrived(codes_ref.at[0, pl.ds(0, sent)], send_sem)


def store_kernel(*refs):
    count = len(refs) // 2
    sem = refs[-1]
    copies = [pltpu.make_async_copy(refs[i], refs[count + i], sem.at[i]) for i in range(count)]
    for copy in copies:
        copy.start()
    for copy in copies:
        copy.wait()


def on_device(bin_codes, node_ids, labels, weights, predictions, f3, b3, f4, b4):
    rows = node_ids.shape[0]
    tiles = rows // LANES
    total_rows = float(rows * lax.axis_size("rows"))
    own = FEATURES // lax.axis_size("feat")
    codes = bin_codes.reshape(FEATURES // 8, 8, tiles, LANES).transpose(0, 2, 1, 3)
    codes = codes.reshape(FEATURES // 8, tiles * 8, LANES)
    dense = [a.reshape(tiles, LANES) for a in (node_ids, labels, weights, predictions)]
    held = pl.BlockSpec(memory_space=pltpu.HBM)
    vmem = pl.BlockSpec(memory_space=pltpu.VMEM)
    outs = pl.pallas_call(
        functools.partial(kernel, total_rows, own),
        name="grow",
        in_specs=[held] * 9,
        out_specs=[vmem] * 5,
        out_shape=[
            jax.ShapeDtypeStruct((own, 2 * NODES3, BINS), F32),
            jax.ShapeDtypeStruct((own, 2 * NODES4, BINS), F32),
            jax.ShapeDtypeStruct((LEAVES,), F32),
            jax.ShapeDtypeStruct((tiles, LANES), F32),
            jax.ShapeDtypeStruct((tiles, LANES), F32),
        ],
        scratch_shapes=[
            pltpu.SMEM((NODES3,), jnp.int32),
            pltpu.SMEM((NODES3,), jnp.int32),
            pltpu.SMEM((NODES4,), jnp.int32),
            pltpu.SMEM((NODES4,), jnp.int32),
            pltpu.VMEM(codes.shape, jnp.int32),
            pltpu.VMEM((tiles, LANES), jnp.int32),
            pltpu.VMEM((tiles, LANES), F32),
            pltpu.VMEM((tiles, LANES), F32),
            pltpu.VMEM((tiles, LANES), F32),
            pltpu.VMEM((own, tiles, LANES), F32),
            pltpu.VMEM((own, tiles, LANES), F32),
            pltpu.VMEM((tiles, LANES), F32),
            pltpu.VMEM((tiles, LANES), F32),
            pltpu.VMEM((tiles, LANES), jnp.int32),
            pltpu.VMEM((tiles, LANES), jnp.int32),
            pltpu.VMEM((tiles, LANES), F32),
            pltpu.VMEM((tiles * 8, LANES), F32),
            pltpu.VMEM((own, 2, 32, LANES), F32),
            pltpu.VMEM((GROUP, own, 8, LANES), F32),
            pltpu.VMEM((own, 8, LANES), F32),
            pltpu.VMEM((GROUP, own, 8, LANES), F32),
            pltpu.VMEM((own, 2, 32, LANES), F32),
            pltpu.VMEM((GROUP, 2, 8, LANES), F32),
            pltpu.VMEM((GROUP, 2, 8, LANES), F32),
            pltpu.VMEM((2, 8, LANES), F32),
            pltpu.VMEM((GROUP, 8, LANES), F32),
            pltpu.VMEM((GROUP, 8, LANES), F32),
            pltpu.VMEM((8, LANES), F32),
            pltpu.SemaphoreType.DMA(()),
            pltpu.SemaphoreType.DMA((3,)),
            pltpu.SemaphoreType.DMA((3,)),
            pltpu.SemaphoreType.DMA((3,)),
            pltpu.SemaphoreType.DMA((2,)),
            pltpu.SemaphoreType.DMA((7,)),
            pltpu.SemaphoreType.DMA((CHUNKS,)),
        ],
        compiler_params=pltpu.CompilerParams(collective_id=0, has_side_effects=True, vmem_limit_bytes=16 << 20),
    )(*[pltpu.with_memory_space_constraint(a, pltpu.HBM) for a in (f3, b3, f4, b4, codes, *dense)])
    anywhere = pl.BlockSpec(memory_space=pl.ANY)
    hist3, hist4, leaf_values, new_pred, new_weight = pl.pallas_call(
        store_kernel,
        name="store",
        in_specs=[anywhere] * len(outs),
        out_specs=[anywhere] * len(outs),
        out_shape=[jax.ShapeDtypeStruct(a.shape, F32) for a in outs],
        scratch_shapes=[pltpu.SemaphoreType.DMA((len(outs),))],
        compiler_params=pltpu.CompilerParams(vmem_limit_bytes=1 << 20),
    )(*outs)
    return hist3, hist4, leaf_values, new_pred.reshape(rows), new_weight.reshape(rows)


def solution(mesh):
    placed = (P(None, "rows"), P("rows"), P("rows"), P("rows"), P("rows"), P(), P(), P(), P())
    return jax.shard_map(
        on_device,
        mesh=mesh,
        in_specs=placed,
        out_specs=(P("feat", None, None), P("feat", None, None), P(), P("rows"), P("rows")),
        check_vma=False,
    )
```

```python
import functools

import jax
import jax.numpy as jnp
from jax import lax
from jax.experimental import pallas as pl
from jax.experimental.pallas import tpu as pltpu
from jax.sharding import PartitionSpec as P

FEATURES = 16
BINS = 256
NODES3 = 8
NODES4 = 16
LEAVES = 32
LANES = 128
CHUNKS = 3
GROUP = 8
GROUP_ORDER = (5, 4, 7, 6, 3, 2, 1)
LINE_ORDER = (5, 6, 7, 4, 3, 2, 1)
MESH = pl.DeviceIdType.MESH
F32 = jnp.float32
BF16 = jnp.bfloat16


def flipped(index, mask):
    out = index
    for bit in (1, 2, 4):
        if mask & bit:
            out = out + bit * (1 - 2 * ((index // bit) % 2))
    return out


def tree_sum(parts):
    while len(parts) > 1:
        parts = [a + b for a, b in zip(parts[::2], parts[1::2])]
    return parts[0]


def kernel(
    total_rows,
    own_features,
    f3_hbm,
    b3_hbm,
    f4_hbm,
    b4_hbm,
    codes_hbm,
    node_hbm,
    label_hbm,
    weight_hbm,
    pred_hbm,
    hist3_ref,
    hist4_ref,
    leaf_value_ref,
    new_pred_ref,
    new_weight_ref,
    f3_ref,
    b3_ref,
    f4_ref,
    b4_ref,
    codes_ref,
    node_ref,
    label_ref,
    weight_ref,
    pred_ref,
    key_ref,
    low_ref,
    wr_ref,
    sr_ref,
    node4_ref,
    leaf_ref,
    leafrow_ref,
    stat_ref,
    acc_ref,
    rs_ref,
    mid_ref,
    ar_ref,
    tot_ref,
    rs_last_ref,
    ar_last_ref,
    mid_last_ref,
    leaf_a_ref,
    leaf_b_ref,
    leaf_mid_ref,
    send_sem,
    rs_sem,
    ar_sem,
    ag_sem,
    leaf_sem,
    in_sem,
    code_sem,
):
    tiles = node_hbm.shape[0]
    steps = tiles // 8
    row = lax.axis_index("rows")
    feat = lax.axis_index("feat")
    group = row % GROUP
    plane = row // GROUP
    in_group = [(plane * GROUP + flipped(group, j), feat) for j in range(1, GROUP)]
    in_line = [(flipped(plane, j) * GROUP + group, feat) for j in range(1, GROUP)]

    def fetch(source, target, sem):
        copy = pltpu.make_async_copy(source, target, sem)
        copy.start()
        return copy

    part = tiles * 8 // CHUNKS
    def fetch_codes(c):
        rows = pl.ds(c * part, part)
        fetch(codes_hbm.at[:, rows], codes_ref.at[:, rows], code_sem.at[c])

    node_ready = fetch(node_hbm, node_ref, in_sem.at[6])
    fetch_codes(0)
    tables = ((f3_hbm, f3_ref), (b3_hbm, b3_ref), (f4_hbm, f4_ref), (b4_hbm, b4_ref))
    ready = [fetch(a, b, in_sem.at[i]) for i, (a, b) in enumerate(tables)]
    for c in range(1, CHUNKS):
        fetch_codes(c)
    for a, b in ((weight_hbm, weight_ref), (label_hbm, label_ref)):
        fetch(a, b, in_sem.at[4])
    pred_ready = fetch(pred_hbm, pred_ref, in_sem.at[5])

    barrier = pltpu.get_barrier_semaphore()
    with jax.named_scope('signal'):
        for peer in in_group + in_line:
            pl.semaphore_signal(barrier, inc=1, device_id=peer, device_id_type=MESH)

    with jax.named_scope('inwait'):
        for copy in ready:
            copy.wait()
        node_ready.wait()

    features3 = [f3_ref[i] for i in range(NODES3)]
    bins3 = [b3_ref[i] for i in range(NODES3)]
    features4 = [f4_ref[i] for i in range(NODES4)]
    bins4 = [b4_ref[i] for i in range(NODES4)]

    def lookup(where_of, tables):
        outs = [jnp.full((8, LANES), table[0], jnp.int32) for table in tables]
        for i in range(1, len(tables[0])):
            hit = where_of == i
            outs = [jnp.where(hit, table[i], out) for table, out in zip(tables, outs)]
        return outs

    def side(step, node_of, features, bins):
        codes = [codes_ref[f // 8, pl.ds(step * 64 + f % 8, 8, stride=8), :] for f in range(FEATURES)]
        chosen, cutoff = lookup(node_of, [features, bins])
        picked = codes[0]
        for f in range(1, FEATURES):
            picked = jnp.where(chosen == f, codes[f], picked)
        return 2 * node_of + jnp.where(picked > cutoff, 1, 0)

    def route(step, carry):
        rows = pl.ds(step * 8, 8)
        node4 = side(step, node_ref[rows, :], features3, bins3)
        node4_ref[rows, :] = node4
        for f in range(own_features):
            index = feat * own_features + f
            code = codes_ref[index // 8, pl.ds(step * 64 + index % 8, 8, stride=8), :]
            low_ref[f, rows, :] = (code & (LANES - 1)).astype(F32)
            key_ref[f, rows, :] = (node4 + NODES4 * (code >> 7)).astype(F32)
        return carry

    def rounding(step, carry):
        rows = pl.ds(step * 8, 8)
        weight = weight_ref[rows, :]
        wr_ref[rows, :] = weight.astype(BF16).astype(F32)
        sr_ref[rows, :] = (weight * label_ref[rows, :]).astype(BF16).astype(F32)
        return carry

    def leaf_route(step, carry):
        rows = pl.ds(step * 8, 8)
        leaf = side(step, node4_ref[rows, :], features4, bins4)
        leaf_ref[rows, :] = leaf
        leafrow_ref[rows, :] = leaf.astype(F32)
        weight = weight_ref[rows, :]
        positive = label_ref[rows, :] > 0.0
        rounded = wr_ref[rows, :]
        rest = weight - rounded
        middle = rest.astype(BF16).astype(F32)
        low = rest - middle
        for j, term in enumerate((rounded, middle, low)):
            stat_ref[pl.ds(step * 64 + j, 8, stride=8), :] = jnp.where(positive, term, 0.0)
            stat_ref[pl.ds(step * 64 + 3 + j, 8, stride=8), :] = jnp.where(positive, 0.0, term)
        for j in (6, 7):
            stat_ref[pl.ds(step * 64 + j, 8, stride=8), :] = jnp.zeros((8, LANES), F32)
        return carry

    def route_piece(c, carry):
        rows = pl.ds(pl.multiple_of(c * part, 8), part)
        pltpu.make_async_copy(codes_hbm.at[:, rows], codes_ref.at[:, rows], code_sem.at[c]).wait()
        first = c * (steps // CHUNKS)
        return lax.fori_loop(0, steps // CHUNKS, lambda i, x: route(first + i, x), carry, unroll=True)

    with jax.named_scope('route'):
        lax.fori_loop(0, CHUNKS, route_piece, 0)
        whole = stat_ref.at[pl.ds(0, 2 * tiles)]
        pltpu.make_async_copy(whole, whole, in_sem.at[4]).wait()
        lax.fori_loop(0, steps, rounding, 0, unroll=True)

    sub = lax.broadcasted_iota(jnp.int32, (16, LANES), 0).astype(F32)
    zero = jnp.zeros((16, LANES), BF16)
    one = jnp.ones((16, LANES), BF16)
    numbers = [(sub + 16 * i).astype(BF16) for i in range(8)]

    def spread(ref, *index):
        return jnp.broadcast_to(ref[index], (16, LANES)).astype(BF16)

    def dot_nt(a, b):
        return lax.dot_general(a, b, (((1,), (1,)), ((), ())), preferred_element_type=F32)

    def leaf_step(step, acc):
        left, right = [], []
        for i in range(8):
            t = step * 8 + i
            left.append(stat_ref[pl.ds(t * 8, 8), :].astype(BF16))
            at = spread(leafrow_ref, pl.ds(t, 1), slice(None))
            right.append(
                jnp.concatenate([jnp.where(at == numbers[k], one, zero) for k in range(2)], axis=0)
            )
        return acc + dot_nt(jnp.concatenate(left, axis=1), jnp.concatenate(right, axis=1))

    def send(source, target, recv, peer):
        pltpu.make_async_remote_copy(
            src_ref=source, dst_ref=target, send_sem=send_sem, recv_sem=recv, device_id=peer, device_id_type=MESH
        ).start()

    def arrived(ref, sem):
        pltpu.make_async_copy(ref, ref, sem).wait()

    others = pl.ds(1, GROUP - 1)

    def tile_of(index):
        return index // 4, pl.ds(pl.multiple_of((index % 4) * 8, 8), 8)

    own_high, own_rows = tile_of(group)

    def leaf_scatter():
        lax.fori_loop(0, steps, leaf_route, 0, unroll=3)
        leaf_sums = lax.fori_loop(0, steps, leaf_step, jnp.zeros((8, LEAVES), F32), unroll=5)
        leaf_a_ref[0, :, :] = jnp.zeros((8, LANES), F32)
        leaf_a_ref[0, :, :LEAVES] = leaf_sums
        for j in GROUP_ORDER:
            send(leaf_a_ref.at[0], leaf_a_ref.at[j], leaf_sem.at[0], in_group[j - 1])

    def leaf_exchange():
        with jax.named_scope('leafwait1'):
            arrived(leaf_a_ref.at[others], leaf_sem.at[0])
        leaf_b_ref[0, :, :] = tree_sum([leaf_a_ref[j] for j in range(GROUP)])
        for j in LINE_ORDER:
            send(leaf_b_ref.at[0], leaf_b_ref.at[j], leaf_sem.at[1], in_line[j - 1])

    def hist_step(f, step, acc):
        left, right = [], []
        for i in range(8):
            t = step * 8 + i
            key = spread(key_ref, f, pl.ds(t, 1), slice(None))
            low = spread(low_ref, f, pl.ds(t, 1), slice(None))
            wr = spread(wr_ref, pl.ds(t, 1), slice(None))
            sr = spread(sr_ref, pl.ds(t, 1), slice(None))
            blocks = []
            for hi in range(2):
                hit = key == numbers[hi]
                blocks += [jnp.where(hit, wr, zero), jnp.where(hit, sr, zero)]
            left.append(jnp.concatenate(blocks, axis=0))
            right.append(
                jnp.concatenate([jnp.where(low == numbers[k], one, zero) for k in range(8)], axis=0)
            )
        return acc + dot_nt(jnp.concatenate(right, axis=1), jnp.concatenate(left, axis=1))

    def compute(f):
        acc = lax.fori_loop(
            0, steps, functools.partial(hist_step, f), jnp.zeros((LANES, 64), F32), unroll=15
        ).T
        acc_ref[f, 0, :, :] = acc[: 2 * NODES4]
        acc_ref[f, 1, :, :] = acc[2 * NODES4 :]

    def scatter(c, first, count):
        some = pl.ds(first, count)
        for j in GROUP_ORDER:
            high, rows = tile_of(flipped(group, j))
            send(acc_ref.at[some, high, rows], rs_ref.at[j, some], rs_sem.at[c], in_group[j - 1])
        rs_ref[0, some, :, :] = acc_ref[some, own_high, own_rows, :]

    def exchange(c, first, count):
        some = pl.ds(first, count)
        with jax.named_scope('rswait'):
            arrived(rs_ref.at[others, some], rs_sem.at[c])
        ar_ref[0, some, :, :] = tree_sum([rs_ref[j, some] for j in range(GROUP)])
        for j in LINE_ORDER:
            send(ar_ref.at[0, some], ar_ref.at[j, some], ar_sem.at[c], in_line[j - 1])

    def gather(c, first, count):
        some = pl.ds(first, count)
        with jax.named_scope('arwait'):
            arrived(ar_ref.at[others, some], ar_sem.at[c])
        mid_ref[some, :, :] = tree_sum([ar_ref[j, some] for j in range(GROUP)])
        for j in GROUP_ORDER:
            send(mid_ref.at[some], tot_ref.at[some, own_high, own_rows], ag_sem.at[c], in_group[j - 1])
        tot_ref[some, own_high, own_rows, :] = mid_ref[some, :, :]

    last = own_features - 1

    def scatter_last():
        for j in GROUP_ORDER:
            _, rows = tile_of(flipped(group, j))
            send(acc_ref.at[last, :, rows], rs_last_ref.at[j], rs_sem.at[2], in_group[j - 1])
        rs_last_ref[0, :, :, :] = acc_ref[last, :, own_rows, :]

    def exchange_last():
        with jax.named_scope('rswait'):
            arrived(rs_last_ref.at[others], rs_sem.at[2])
        ar_last_ref[0, :, :, :] = tree_sum([rs_last_ref[j] for j in range(GROUP)])
        for j in LINE_ORDER:
            send(ar_last_ref.at[0], ar_last_ref.at[j], ar_sem.at[2], in_line[j - 1])

    def gather_last():
        near = [flipped(group, j) for j in (3, 2)]
        near.append(flipped(group, 1))
        with jax.named_scope('arwait'):
            arrived(ar_last_ref.at[others], ar_sem.at[2])
        mid_last_ref[...] = tree_sum([ar_last_ref[j] for j in range(GROUP)])
        for peer in near:
            send(mid_last_ref, tot_ref.at[last, :, own_rows], ag_sem.at[2], (plane * GROUP + peer, feat))
        tot_ref[last, :, own_rows, :] = mid_last_ref[...]

    with jax.named_scope('compute'):
        compute(0)
        compute(1)
    with jax.named_scope('barwait'):
        pl.semaphore_wait(barrier, 2 * (GROUP - 1))
    scatter(0, 0, 2)

    def grow_one(f, carry):
        with jax.named_scope('compute'):
            compute(f)

        @pl.when(f < last)
        def _():
            scatter(1, 2, 1)

        @pl.when(f == last)
        def _():
            scatter_last()

        return carry

    lax.fori_loop(2, own_features, grow_one, 0)
    batches = ((0, 0, 2), (1, 2, 1))
    exchange(*batches[0])
    with jax.named_scope('leaf_scatter'):
        leaf_scatter()
    exchange(*batches[1])
    exchange_last()
    leaf_exchange()
    for batch in batches:
        gather(*batch)
    gather_last()
    with jax.named_scope('leafwait2'):
        arrived(leaf_b_ref.at[others], leaf_sem.at[1])
    leaf_mid_ref[...] = tree_sum([leaf_b_ref[j] for j in range(GROUP)])
    plus = leaf_mid_ref[0:1, :]
    minus = leaf_mid_ref[3:4, :]
    values = (plus - minus) / ((plus + minus) + 1.0)
    leaf_value_ref[...] = values[0, :LEAVES]
    all_plus = plus + (leaf_mid_ref[1:2, :] + leaf_mid_ref[2:3, :])
    all_minus = minus + (leaf_mid_ref[4:5, :] + leaf_mid_ref[5:6, :])
    grand = jnp.sum(all_plus * jnp.exp(-values) + all_minus * jnp.exp(values), axis=1, keepdims=True)
    scale = jnp.broadcast_to(total_rows / grand, (8, LANES))
    table = jnp.broadcast_to(values, (8, LANES))

    def update(step, carry):
        rows = pl.ds(step * 8, 8)
        stepped = jnp.take_along_axis(table, leaf_ref[rows, :], axis=1)
        new_pred_ref[rows, :] = pred_ref[rows, :] + stepped
        raw = weight_ref[rows, :] * jnp.exp(-label_ref[rows, :] * stepped)
        new_weight_ref[rows, :] = raw * scale
        return carry

    pred_ready.wait()
    with jax.named_scope('update'):
        lax.fori_loop(0, steps, update, 0, unroll=5)

    def store(f):
        for hi in range(2):
            lanes = slice(hi * LANES, (hi + 1) * LANES)
            hist4_ref[f, :, lanes] = tot_ref[f, hi]
            even = tot_ref[f, hi, pl.ds(0, 2 * NODES3, stride=2), :]
            odd = tot_ref[f, hi, pl.ds(1, 2 * NODES3, stride=2), :]
            hist3_ref[f, :, lanes] = even + odd

    for c, first, count in batches:
        with jax.named_scope('agwait'):
            whole = stat_ref.at[pl.ds(0, count * 8 * (GROUP - 1))]
            arrived(whole, ag_sem.at[c])
        for f in range(first, first + count):
            store(f)
    with jax.named_scope('agwait'):
        arrived(tot_ref.at[last, :, pl.ds(0, 24)], ag_sem.at[2])
    store(last)
    tiles_sent = (3 * last + 2) * (GROUP - 1) + 2 * (2 * (GROUP - 1) + 3)
    sent = tiles_sent * 8
    with jax.named_scope('sendwait'):
        arrived(codes_ref.at[0, pl.ds(0, sent)], send_sem)


def store_kernel(*refs):
    count = len(refs) // 2
    sem = refs[-1]
    copies = [pltpu.make_async_copy(refs[i], refs[count + i], sem.at[i]) for i in range(count)]
    for copy in copies:
        copy.start()
    for copy in copies:
        copy.wait()


def on_device(bin_codes, node_ids, labels, weights, predictions, f3, b3, f4, b4):
    rows = node_ids.shape[0]
    tiles = rows // LANES
    total_rows = float(rows * lax.axis_size("rows"))
    own = FEATURES // lax.axis_size("feat")
    codes = bin_codes.reshape(FEATURES // 8, 8, tiles, LANES).transpose(0, 2, 1, 3)
    codes = codes.reshape(FEATURES // 8, tiles * 8, LANES)
    dense = [a.reshape(tiles, LANES) for a in (node_ids, labels, weights, predictions)]
    held = pl.BlockSpec(memory_space=pltpu.HBM)
    vmem = pl.BlockSpec(memory_space=pltpu.VMEM)
    outs = pl.pallas_call(
        functools.partial(kernel, total_rows, own),
        name="grow",
        in_specs=[held] * 9,
        out_specs=[vmem] * 5,
        out_shape=[
            jax.ShapeDtypeStruct((own, 2 * NODES3, BINS), F32),
            jax.ShapeDtypeStruct((own, 2 * NODES4, BINS), F32),
            jax.ShapeDtypeStruct((LEAVES,), F32),
            jax.ShapeDtypeStruct((tiles, LANES), F32),
            jax.ShapeDtypeStruct((tiles, LANES), F32),
        ],
        scratch_shapes=[
            pltpu.SMEM((NODES3,), jnp.int32),
            pltpu.SMEM((NODES3,), jnp.int32),
            pltpu.SMEM((NODES4,), jnp.int32),
            pltpu.SMEM((NODES4,), jnp.int32),
            pltpu.VMEM(codes.shape, jnp.int32),
            pltpu.VMEM((tiles, LANES), jnp.int32),
            pltpu.VMEM((tiles, LANES), F32),
            pltpu.VMEM((tiles, LANES), F32),
            pltpu.VMEM((tiles, LANES), F32),
            pltpu.VMEM((own, tiles, LANES), F32),
            pltpu.VMEM((own, tiles, LANES), F32),
            pltpu.VMEM((tiles, LANES), F32),
            pltpu.VMEM((tiles, LANES), F32),
            pltpu.VMEM((tiles, LANES), jnp.int32),
            pltpu.VMEM((tiles, LANES), jnp.int32),
            pltpu.VMEM((tiles, LANES), F32),
            pltpu.VMEM((tiles * 8, LANES), F32),
            pltpu.VMEM((own, 2, 32, LANES), F32),
            pltpu.VMEM((GROUP, own, 8, LANES), F32),
            pltpu.VMEM((own, 8, LANES), F32),
            pltpu.VMEM((GROUP, own, 8, LANES), F32),
            pltpu.VMEM((own, 2, 32, LANES), F32),
            pltpu.VMEM((GROUP, 2, 8, LANES), F32),
            pltpu.VMEM((GROUP, 2, 8, LANES), F32),
            pltpu.VMEM((2, 8, LANES), F32),
            pltpu.VMEM((GROUP, 8, LANES), F32),
            pltpu.VMEM((GROUP, 8, LANES), F32),
            pltpu.VMEM((8, LANES), F32),
            pltpu.SemaphoreType.DMA(()),
            pltpu.SemaphoreType.DMA((3,)),
            pltpu.SemaphoreType.DMA((3,)),
            pltpu.SemaphoreType.DMA((3,)),
            pltpu.SemaphoreType.DMA((2,)),
            pltpu.SemaphoreType.DMA((7,)),
            pltpu.SemaphoreType.DMA((CHUNKS,)),
        ],
        compiler_params=pltpu.CompilerParams(collective_id=0, has_side_effects=True, vmem_limit_bytes=16 << 20),
    )(*[pltpu.with_memory_space_constraint(a, pltpu.HBM) for a in (f3, b3, f4, b4, codes, *dense)])
    anywhere = pl.BlockSpec(memory_space=pl.ANY)
    hist3, hist4, leaf_values, new_pred, new_weight = pl.pallas_call(
        store_kernel,
        name="store",
        in_specs=[anywhere] * len(outs),
        out_specs=[anywhere] * len(outs),
        out_shape=[jax.ShapeDtypeStruct(a.shape, F32) for a in outs],
        scratch_shapes=[pltpu.SemaphoreType.DMA((len(outs),))],
        compiler_params=pltpu.CompilerParams(vmem_limit_bytes=1 << 20),
    )(*outs)
    return hist3, hist4, leaf_values, new_pred.reshape(rows), new_weight.reshape(rows)


def solution(mesh):
    placed = (P(None, "rows"), P("rows"), P("rows"), P("rows"), P("rows"), P(), P(), P(), P())
    return jax.shard_map(
        on_device,
        mesh=mesh,
        in_specs=placed,
        out_specs=(P("feat", None, None), P("feat", None, None), P(), P("rows"), P("rows")),
        check_vma=False,
    )
```

```python
import functools

import jax
import jax.numpy as jnp
from jax import lax
from jax.experimental import pallas as pl
from jax.experimental.pallas import tpu as pltpu
from jax.sharding import PartitionSpec as P

FEATURES = 16
BINS = 256
NODES3 = 8
NODES4 = 16
LEAVES = 32
LANES = 128
CHUNKS = 3
GROUP = 8
GROUP_ORDER = (5, 4, 7, 6, 3, 2, 1)
LINE_ORDER = (5, 6, 7, 4, 3, 2, 1)
MESH = pl.DeviceIdType.MESH
F32 = jnp.float32
BF16 = jnp.bfloat16


def flipped(index, mask):
    out = index
    for bit in (1, 2, 4):
        if mask & bit:
            out = out + bit * (1 - 2 * ((index // bit) % 2))
    return out


def tree_sum(parts):
    while len(parts) > 1:
        parts = [a + b for a, b in zip(parts[::2], parts[1::2])]
    return parts[0]


def kernel(
    total_rows,
    own_features,
    f3_hbm,
    b3_hbm,
    f4_hbm,
    b4_hbm,
    codes_hbm,
    node_hbm,
    label_hbm,
    weight_hbm,
    pred_hbm,
    hist3_ref,
    hist4_ref,
    leaf_value_ref,
    new_pred_ref,
    new_weight_ref,
    f3_ref,
    b3_ref,
    f4_ref,
    b4_ref,
    codes_ref,
    node_ref,
    label_ref,
    weight_ref,
    pred_ref,
    key_ref,
    low_ref,
    wr_ref,
    sr_ref,
    node4_ref,
    leaf_ref,
    leafrow_ref,
    stat_ref,
    acc_ref,
    rs_ref,
    mid_ref,
    ar_ref,
    tot_ref,
    rs_last_ref,
    ar_last_ref,
    mid_last_ref,
    leaf_a_ref,
    leaf_b_ref,
    leaf_mid_ref,
    rs_sem,
    ar_sem,
    ag_sem,
    leaf_sem,
    in_sem,
    code_sem,
):
    tiles = node_hbm.shape[0]
    steps = tiles // 8
    row = lax.axis_index("rows")
    feat = lax.axis_index("feat")
    group = row % GROUP
    plane = row // GROUP
    in_group = [(plane * GROUP + flipped(group, j), feat) for j in range(1, GROUP)]
    in_line = [(flipped(plane, j) * GROUP + group, feat) for j in range(1, GROUP)]

    def fetch(source, target, sem):
        copy = pltpu.make_async_copy(source, target, sem)
        copy.start()
        return copy

    part = tiles * 8 // CHUNKS
    def fetch_codes(c):
        rows = pl.ds(c * part, part)
        fetch(codes_hbm.at[:, rows], codes_ref.at[:, rows], code_sem.at[c])

    node_ready = fetch(node_hbm, node_ref, in_sem.at[5])
    fetch_codes(0)
    tables = ((f3_hbm, f3_ref), (b3_hbm, b3_ref), (f4_hbm, f4_ref), (b4_hbm, b4_ref))
    ready = [fetch(a, b, in_sem.at[i]) for i, (a, b) in enumerate(tables)]
    for c in range(1, CHUNKS):
        fetch_codes(c)
    for a, b in ((weight_hbm, weight_ref), (label_hbm, label_ref)):
        fetch(a, b, in_sem.at[4])

    barrier = pltpu.get_barrier_semaphore()
    with jax.named_scope('signal'):
        for peer in in_group + in_line:
            pl.semaphore_signal(barrier, inc=1, device_id=peer, device_id_type=MESH)

    with jax.named_scope('inwait'):
        for copy in ready:
            copy.wait()
        node_ready.wait()

    features3 = [f3_ref[i] for i in range(NODES3)]
    bins3 = [b3_ref[i] for i in range(NODES3)]
    features4 = [f4_ref[i] for i in range(NODES4)]
    bins4 = [b4_ref[i] for i in range(NODES4)]

    def lookup(where_of, tables):
        outs = [jnp.full((8, LANES), table[0], jnp.int32) for table in tables]
        for i in range(1, len(tables[0])):
            hit = where_of == i
            outs = [jnp.where(hit, table[i], out) for table, out in zip(tables, outs)]
        return outs

    def side(step, node_of, features, bins):
        codes = [codes_ref[f // 8, pl.ds(step * 64 + f % 8, 8, stride=8), :] for f in range(FEATURES)]
        chosen, cutoff = lookup(node_of, [features, bins])
        picked = codes[0]
        for f in range(1, FEATURES):
            picked = jnp.where(chosen == f, codes[f], picked)
        return 2 * node_of + jnp.where(picked > cutoff, 1, 0)

    def route(step, carry):
        rows = pl.ds(step * 8, 8)
        node4 = side(step, node_ref[rows, :], features3, bins3)
        node4_ref[rows, :] = node4
        for f in range(own_features):
            index = feat * own_features + f
            code = codes_ref[index // 8, pl.ds(step * 64 + index % 8, 8, stride=8), :]
            low_ref[f, rows, :] = (code & (LANES - 1)).astype(F32)
            key_ref[f, rows, :] = (node4 + NODES4 * (code >> 7)).astype(F32)
        return carry

    def rounding(step, carry):
        rows = pl.ds(step * 8, 8)
        weight = weight_ref[rows, :]
        wr_ref[rows, :] = weight.astype(BF16).astype(F32)
        sr_ref[rows, :] = (weight * label_ref[rows, :]).astype(BF16).astype(F32)
        return carry

    def leaf_route(step, carry):
        rows = pl.ds(step * 8, 8)
        leaf = side(step, node4_ref[rows, :], features4, bins4)
        leaf_ref[rows, :] = leaf
        leafrow_ref[rows, :] = leaf.astype(F32)
        weight = weight_ref[rows, :]
        positive = label_ref[rows, :] > 0.0
        rounded = wr_ref[rows, :]
        rest = weight - rounded
        middle = rest.astype(BF16).astype(F32)
        low = rest - middle
        for j, term in enumerate((rounded, middle, low)):
            stat_ref[pl.ds(step * 64 + j, 8, stride=8), :] = jnp.where(positive, term, 0.0)
            stat_ref[pl.ds(step * 64 + 3 + j, 8, stride=8), :] = jnp.where(positive, 0.0, term)
        for j in (6, 7):
            stat_ref[pl.ds(step * 64 + j, 8, stride=8), :] = jnp.zeros((8, LANES), F32)
        return carry

    def route_piece(c, carry):
        rows = pl.ds(pl.multiple_of(c * part, 8), part)
        pltpu.make_async_copy(codes_hbm.at[:, rows], codes_ref.at[:, rows], code_sem.at[c]).wait()
        first = c * (steps // CHUNKS)
        return lax.fori_loop(0, steps // CHUNKS, lambda i, x: route(first + i, x), carry, unroll=True)

    with jax.named_scope('route'):
        lax.fori_loop(0, CHUNKS, route_piece, 0)
        whole = stat_ref.at[pl.ds(0, 2 * tiles)]
        pltpu.make_async_copy(whole, whole, in_sem.at[4]).wait()
        lax.fori_loop(0, steps, rounding, 0, unroll=True)
    pred_ready = fetch(pred_hbm, pred_ref, in_sem.at[5])

    sub = lax.broadcasted_iota(jnp.int32, (16, LANES), 0).astype(F32)
    zero = jnp.zeros((16, LANES), BF16)
    one = jnp.ones((16, LANES), BF16)
    numbers = [(sub + 16 * i).astype(BF16) for i in range(8)]

    def spread(ref, *index):
        return jnp.broadcast_to(ref[index], (16, LANES)).astype(BF16)

    def dot_nt(a, b):
        return lax.dot_general(a, b, (((1,), (1,)), ((), ())), preferred_element_type=F32)

    def leaf_step(step, acc):
        left, right = [], []
        for i in range(8):
            t = step * 8 + i
            left.append(stat_ref[pl.ds(t * 8, 8), :].astype(BF16))
            at = spread(leafrow_ref, pl.ds(t, 1), slice(None))
            right.append(
                jnp.concatenate([jnp.where(at == numbers[k], one, zero) for k in range(2)], axis=0)
            )
        return acc + dot_nt(jnp.concatenate(left, axis=1), jnp.concatenate(right, axis=1))

    def send(source, target, recv, peer):
        pltpu.make_async_remote_copy(
            src_ref=source, dst_ref=target, send_sem=code_sem.at[0], recv_sem=recv, device_id=peer, device_id_type=MESH
        ).start()

    def arrived(ref, sem):
        pltpu.make_async_copy(ref, ref, sem).wait()

    others = pl.ds(1, GROUP - 1)

    def tile_of(index):
        return index // 4, pl.ds(pl.multiple_of((index % 4) * 8, 8), 8)

    own_high, own_rows = tile_of(group)

    def leaf_scatter():
        lax.fori_loop(0, steps, leaf_route, 0, unroll=3)
        leaf_sums = lax.fori_loop(0, steps, leaf_step, jnp.zeros((8, LEAVES), F32), unroll=5)
        leaf_a_ref[0, :, :] = jnp.zeros((8, LANES), F32)
        leaf_a_ref[0, :, :LEAVES] = leaf_sums
        for j in GROUP_ORDER:
            send(leaf_a_ref.at[0], leaf_a_ref.at[j], leaf_sem.at[0], in_group[j - 1])

    def leaf_exchange():
        with jax.named_scope('leafwait1'):
            arrived(leaf_a_ref.at[others], leaf_sem.at[0])
        leaf_b_ref[0, :, :] = tree_sum([leaf_a_ref[j] for j in range(GROUP)])
        for j in LINE_ORDER:
            send(leaf_b_ref.at[0], leaf_b_ref.at[j], leaf_sem.at[1], in_line[j - 1])

    def hist_step(f, step, acc):
        left, right = [], []
        for i in range(8):
            t = step * 8 + i
            key = spread(key_ref, f, pl.ds(t, 1), slice(None))
            low = spread(low_ref, f, pl.ds(t, 1), slice(None))
            wr = spread(wr_ref, pl.ds(t, 1), slice(None))
            sr = spread(sr_ref, pl.ds(t, 1), slice(None))
            blocks = []
            for hi in range(2):
                hit = key == numbers[hi]
                blocks += [jnp.where(hit, wr, zero), jnp.where(hit, sr, zero)]
            left.append(jnp.concatenate(blocks, axis=0))
            right.append(
                jnp.concatenate([jnp.where(low == numbers[k], one, zero) for k in range(8)], axis=0)
            )
        return acc + dot_nt(jnp.concatenate(right, axis=1), jnp.concatenate(left, axis=1))

    def compute(f):
        acc = lax.fori_loop(
            0, steps, functools.partial(hist_step, f), jnp.zeros((LANES, 64), F32), unroll=15
        ).T
        acc_ref[f, 0, :, :] = acc[: 2 * NODES4]
        acc_ref[f, 1, :, :] = acc[2 * NODES4 :]

    def scatter(c, first, count):
        some = pl.ds(first, count)
        for j in GROUP_ORDER:
            high, rows = tile_of(flipped(group, j))
            send(acc_ref.at[some, high, rows], rs_ref.at[j, some], rs_sem.at[c], in_group[j - 1])
        rs_ref[0, some, :, :] = acc_ref[some, own_high, own_rows, :]

    def exchange(c, first, count):
        some = pl.ds(first, count)
        with jax.named_scope('rswait'):
            arrived(rs_ref.at[others, some], rs_sem.at[c])
        ar_ref[0, some, :, :] = tree_sum([rs_ref[j, some] for j in range(GROUP)])
        for j in LINE_ORDER:
            send(ar_ref.at[0, some], ar_ref.at[j, some], ar_sem.at[c], in_line[j - 1])

    def gather(c, first, count):
        some = pl.ds(first, count)
        with jax.named_scope('arwait'):
            arrived(ar_ref.at[others, some], ar_sem.at[c])
        mid_ref[some, :, :] = tree_sum([ar_ref[j, some] for j in range(GROUP)])
        for j in GROUP_ORDER:
            send(mid_ref.at[some], tot_ref.at[some, own_high, own_rows], ag_sem.at[0], in_group[j - 1])
        tot_ref[some, own_high, own_rows, :] = mid_ref[some, :, :]

    last = own_features - 1

    def scatter_last():
        for j in GROUP_ORDER:
            _, rows = tile_of(flipped(group, j))
            send(acc_ref.at[last, :, rows], rs_last_ref.at[j], rs_sem.at[2], in_group[j - 1])
        rs_last_ref[0, :, :, :] = acc_ref[last, :, own_rows, :]

    def exchange_last():
        with jax.named_scope('rswait'):
            arrived(rs_last_ref.at[others], rs_sem.at[2])
        ar_last_ref[0, :, :, :] = tree_sum([rs_last_ref[j] for j in range(GROUP)])
        for j in LINE_ORDER:
            send(ar_last_ref.at[0], ar_last_ref.at[j], ar_sem.at[2], in_line[j - 1])

    def gather_last():
        near = [flipped(group, j) for j in (3, 2)]
        near.append(flipped(group, 1))
        with jax.named_scope('arwait'):
            arrived(ar_last_ref.at[others], ar_sem.at[2])
        mid_last_ref[...] = tree_sum([ar_last_ref[j] for j in range(GROUP)])
        for peer in near:
            send(mid_last_ref, tot_ref.at[last, :, own_rows], ag_sem.at[1], (plane * GROUP + peer, feat))
        tot_ref[last, :, own_rows, :] = mid_last_ref[...]

    with jax.named_scope('compute'):
        compute(0)
        compute(1)
    with jax.named_scope('barwait'):
        pl.semaphore_wait(barrier, 2 * (GROUP - 1))
    scatter(0, 0, 2)

    def grow_one(f, carry):
        with jax.named_scope('compute'):
            compute(f)

        @pl.when(f < last)
        def _():
            scatter(1, 2, 1)

        @pl.when(f == last)
        def _():
            scatter_last()

        return carry

    lax.fori_loop(2, own_features, grow_one, 0)
    batches = ((0, 0, 2), (1, 2, 1))
    exchange(*batches[0])
    with jax.named_scope('leaf_scatter'):
        leaf_scatter()
    exchange(*batches[1])
    exchange_last()
    leaf_exchange()
    for batch in batches:
        gather(*batch)
    gather_last()
    with jax.named_scope('leafwait2'):
        arrived(leaf_b_ref.at[others], leaf_sem.at[1])
    leaf_mid_ref[...] = tree_sum([leaf_b_ref[j] for j in range(GROUP)])
    plus = leaf_mid_ref[0:1, :]
    minus = leaf_mid_ref[3:4, :]
    values = (plus - minus) / ((plus + minus) + 1.0)
    leaf_value_ref[...] = values[0, :LEAVES]
    all_plus = plus + (leaf_mid_ref[1:2, :] + leaf_mid_ref[2:3, :])
    all_minus = minus + (leaf_mid_ref[4:5, :] + leaf_mid_ref[5:6, :])
    grand = jnp.sum(all_plus * jnp.exp(-values) + all_minus * jnp.exp(values), axis=1, keepdims=True)
    scale = jnp.broadcast_to(total_rows / grand, (8, LANES))
    table = jnp.broadcast_to(values, (8, LANES))

    def update(step, carry):
        rows = pl.ds(step * 8, 8)
        stepped = jnp.take_along_axis(table, leaf_ref[rows, :], axis=1)
        new_pred_ref[rows, :] = pred_ref[rows, :] + stepped
        raw = weight_ref[rows, :] * jnp.exp(-label_ref[rows, :] * stepped)
        new_weight_ref[rows, :] = raw * scale
        return carry

    pred_ready.wait()
    with jax.named_scope('update'):
        lax.fori_loop(0, steps, update, 0, unroll=5)

    def store(f):
        for hi in range(2):
            lanes = slice(hi * LANES, (hi + 1) * LANES)
            hist4_ref[f, :, lanes] = tot_ref[f, hi]
            even = tot_ref[f, hi, pl.ds(0, 2 * NODES3, stride=2), :]
            odd = tot_ref[f, hi, pl.ds(1, 2 * NODES3, stride=2), :]
            hist3_ref[f, :, lanes] = even + odd

    with jax.named_scope('agwait'):
        arrived(stat_ref.at[pl.ds(0, last * 8 * (GROUP - 1))], ag_sem.at[0])
    for f in range(last):
        store(f)
    with jax.named_scope('agwait'):
        arrived(tot_ref.at[last, :, pl.ds(0, 24)], ag_sem.at[1])
    store(last)
    tiles_sent = (3 * last + 2) * (GROUP - 1) + 2 * (2 * (GROUP - 1) + 3)
    sent = tiles_sent * 8
    with jax.named_scope('sendwait'):
        arrived(codes_ref.at[0, pl.ds(0, sent)], code_sem.at[0])


def store_kernel(*refs):
    count = len(refs) // 2
    sem = refs[-1]
    copies = [pltpu.make_async_copy(refs[i], refs[count + i], sem.at[i]) for i in range(count)]
    for copy in copies:
        copy.start()
    for copy in copies:
        copy.wait()


def on_device(bin_codes, node_ids, labels, weights, predictions, f3, b3, f4, b4):
    rows = node_ids.shape[0]
    tiles = rows // LANES
    total_rows = float(rows * lax.axis_size("rows"))
    own = FEATURES // lax.axis_size("feat")
    codes = bin_codes.reshape(FEATURES // 8, 8, tiles, LANES).transpose(0, 2, 1, 3)
    codes = codes.reshape(FEATURES // 8, tiles * 8, LANES)
    dense = [a.reshape(tiles, LANES) for a in (node_ids, labels, weights, predictions)]
    held = pl.BlockSpec(memory_space=pltpu.HBM)
    vmem = pl.BlockSpec(memory_space=pltpu.VMEM)
    outs = pl.pallas_call(
        functools.partial(kernel, total_rows, own),
        name="grow",
        in_specs=[held] * 9,
        out_specs=[vmem] * 5,
        out_shape=[
            jax.ShapeDtypeStruct((own, 2 * NODES3, BINS), F32),
            jax.ShapeDtypeStruct((own, 2 * NODES4, BINS), F32),
            jax.ShapeDtypeStruct((LEAVES,), F32),
            jax.ShapeDtypeStruct((tiles, LANES), F32),
            jax.ShapeDtypeStruct((tiles, LANES), F32),
        ],
        scratch_shapes=[
            pltpu.SMEM((NODES3,), jnp.int32),
            pltpu.SMEM((NODES3,), jnp.int32),
            pltpu.SMEM((NODES4,), jnp.int32),
            pltpu.SMEM((NODES4,), jnp.int32),
            pltpu.VMEM(codes.shape, jnp.int32),
            pltpu.VMEM((tiles, LANES), jnp.int32),
            pltpu.VMEM((tiles, LANES), F32),
            pltpu.VMEM((tiles, LANES), F32),
            pltpu.VMEM((tiles, LANES), F32),
            pltpu.VMEM((own, tiles, LANES), F32),
            pltpu.VMEM((own, tiles, LANES), F32),
            pltpu.VMEM((tiles, LANES), F32),
            pltpu.VMEM((tiles, LANES), F32),
            pltpu.VMEM((tiles, LANES), jnp.int32),
            pltpu.VMEM((tiles, LANES), jnp.int32),
            pltpu.VMEM((tiles, LANES), F32),
            pltpu.VMEM((tiles * 8, LANES), F32),
            pltpu.VMEM((own, 2, 32, LANES), F32),
            pltpu.VMEM((GROUP, own, 8, LANES), F32),
            pltpu.VMEM((own, 8, LANES), F32),
            pltpu.VMEM((GROUP, own, 8, LANES), F32),
            pltpu.VMEM((own, 2, 32, LANES), F32),
            pltpu.VMEM((GROUP, 2, 8, LANES), F32),
            pltpu.VMEM((GROUP, 2, 8, LANES), F32),
            pltpu.VMEM((2, 8, LANES), F32),
            pltpu.VMEM((GROUP, 8, LANES), F32),
            pltpu.VMEM((GROUP, 8, LANES), F32),
            pltpu.VMEM((8, LANES), F32),
            pltpu.SemaphoreType.DMA((3,)),
            pltpu.SemaphoreType.DMA((3,)),
            pltpu.SemaphoreType.DMA((2,)),
            pltpu.SemaphoreType.DMA((2,)),
            pltpu.SemaphoreType.DMA((6,)),
            pltpu.SemaphoreType.DMA((CHUNKS,)),
        ],
        compiler_params=pltpu.CompilerParams(collective_id=0, has_side_effects=True, vmem_limit_bytes=16 << 20),
    )(*[pltpu.with_memory_space_constraint(a, pltpu.HBM) for a in (f3, b3, f4, b4, codes, *dense)])
    anywhere = pl.BlockSpec(memory_space=pl.ANY)
    hist3, hist4, leaf_values, new_pred, new_weight = pl.pallas_call(
        store_kernel,
        name="store",
        in_specs=[anywhere] * len(outs),
        out_specs=[anywhere] * len(outs),
        out_shape=[jax.ShapeDtypeStruct(a.shape, F32) for a in outs],
        scratch_shapes=[pltpu.SemaphoreType.DMA((len(outs),))],
        compiler_params=pltpu.CompilerParams(vmem_limit_bytes=1 << 20),
    )(*outs)
    return hist3, hist4, leaf_values, new_pred.reshape(rows), new_weight.reshape(rows)


def solution(mesh):
    placed = (P(None, "rows"), P("rows"), P("rows"), P("rows"), P("rows"), P(), P(), P(), P())
    return jax.shard_map(
        on_device,
        mesh=mesh,
        in_specs=placed,
        out_specs=(P("feat", None, None), P("feat", None, None), P(), P("rows"), P("rows")),
        check_vma=False,
    )
```
